128 devices in a mesh: sec: 2 (over y_lo), dev: 64 (over x, y_hi, z, core).
Axes of the slice: x: 4, y: 4 (y_hi: 2, y_lo: 2; y = y_hi * 2 + y_lo), z: 4, core: 2. Of those that a mesh axis runs over, the one named last changes fastest.
Arguments:
- hidden_in: bfloat16 [4096, 4096], P(('sec', 'dev')), may hold values from -6 to 6
- routes: int32 [4096, 8], P(('sec', 'dev')), may hold values from 0 to 63, all different within a row; in each aligned block of 32 rows (0 to 31, 32 to 63, ...) at most 8 rows name the same one
- scores: float32 [4096, 8], P(('sec', 'dev')), may hold values from 0.05 to 1
- w_gate: bfloat16 [64, 4096, 1536], P('dev', None, 'sec'), may hold values from -0.09375 to 0.09375
- w_up: bfloat16 [64, 4096, 1536], P('dev', None, 'sec'), may hold values from -0.09375 to 0.09375
- w_down: bfloat16 [64, 1536, 4096], P('dev', 'sec'), may hold values from -0.15625 to 0.15625
Outputs:
- mixed: bfloat16 [4096, 4096], P(('sec', 'dev'))
The draws below stay inside these ranges and needn't reach their ends.
Inputs may be any that keep to these rules, and one draw needn't show every extreme that they name: `routes`: each row names 8 different experts; among the rows of one device no expert is named by more than 8 rows, and in every draw some expert is named by exactly 8 rows of some device.
All inputs are finite; a program needn't handle non-finite values.
Results may differ from the reference program's by a relative error of at most 0.017.
Values may be sent and summed in bfloat16 or wider, within the bound.
A program may use at most 128 MiB of HBM per device.

```python
import math
import jax
import jax.numpy as jnp
import numpy as np
from jax import lax

D = 4096
FF = 1536
TOP = 8
ROWS_DEV = 32
EXPERTS = 64
CAP = 8
TOKENS = 4096
N_SEC = 2
N_DEV = 64


def shard_levels(stream_key, dims, shards, low, top_value):
    gain = 1.0
    for axis_at, shards_of in shards:
        heights = jax.random.uniform(jax.random.fold_in(jax.random.fold_in(stream_key, 6), axis_at), (shards_of,), jnp.float32, low / len(shards), top_value / len(shards))
        gain = gain * jnp.repeat(jnp.exp(heights), dims[axis_at] // shards_of).reshape((-1,) + (1,) * (len(dims) - 1 - axis_at))
    return gain


def deal_out(stream_key, own, number, rows, amount, top, most, skew):
    sequence = jax.random.permutation(stream_key, amount)
    crowded, usual = portions_of(amount, rows * top, most, skew, True), portions_of(amount, rows * top, most, skew, False)
    places = jnp.arange(amount)

    def named(lengths, offset_by):
        used = int((lengths > 0).sum())
        fixed = max(1, used // 4)
        passed = fixed + (places - fixed + offset_by * (used - fixed)) % max(1, amount - fixed)
        return jnp.zeros((amount,), jnp.int32).at[sequence[jnp.where(places < fixed, places, passed)]].set(jnp.asarray(lengths, jnp.int32))

    lengths = jnp.where(number % 4 == 0, named(crowded, number // 4), named(usual, number - number // 4 - 1))
    mixed = jax.random.permutation(jax.random.fold_in(own, 3), amount)
    donor, receiver = mixed[0:amount // 2 * 2:2], mixed[1:amount // 2 * 2:2]
    room = jnp.minimum(lengths[donor] - 1, most - lengths[receiver]) // 2
    room = jnp.where((donor == sequence[0]) | (receiver == sequence[0]) | (lengths[receiver] == 0), 0, jnp.maximum(room, 0))
    passed = jax.random.randint(jax.random.fold_in(own, 4), (amount // 2,), 0, 1 << 20) % (room + 1)
    lengths = lengths.at[donor].add(-passed).at[receiver].add(passed)
    members = jnp.searchsorted(jnp.cumsum(lengths), jnp.arange(rows * top), side="right").astype(jnp.int32)
    grid = members.reshape(top, rows).T
    grid = grid[jax.random.permutation(jax.random.fold_in(own, 1), rows)]
    offset_by = jax.random.randint(jax.random.fold_in(own, 2), (rows, 1), 0, top)
    return jnp.take_along_axis(grid, (jnp.arange(top)[None, :] + offset_by) % top, axis=1)


def portions_of(amount, total, bound, skew, full):
    weights = [(1 << 20) // math.isqrt(standing ** skew) + 1 for standing in range(1, amount + 1)]
    largest = bound if full else min(bound, max(-(-total // amount), total * weights[0] // sum(weights)))
    least = 1 if total - largest >= amount - 1 else 0
    holding, rest = [largest] + [least] * (amount - 1), total - largest - least * (amount - 1)
    while rest > 0:
        free = [i for i in range(1, amount) if holding[i] < largest] or [i for i in range(1, amount) if holding[i] < bound]
        mass, remaining = sum([weights[i] for i in free]), rest
        for i in free:
            addition = min(bound - holding[i], max(1, remaining * weights[i] // mass), rest)
            holding[i] = holding[i] + addition
            rest = rest - addition
    return np.array(holding)


def centred(key, extent, spread, reach, shards=(), kind=jnp.bfloat16):
    loudness = shard_levels(key, extent, shards, -0.22, 0.18) if shards else 1.0
    values = jax.random.normal(key, extent, jnp.float32) * spread * loudness
    return jnp.minimum(jnp.maximum(values, -reach), reach).astype(kind)


def setup_inputs(seed: int = 0) -> dict:
    splits = jax.random.split(jax.random.key(seed), 7)
    hidden_in = centred(splits[0], (TOKENS, D), 1.0, 6.0, ((0, 128),))
    routes_keys = jax.random.split(jax.random.fold_in(splits[1], 1), TOKENS // ROWS_DEV)
    routes_turns = jax.random.permutation(jax.random.fold_in(splits[1], 3), TOKENS // ROWS_DEV)
    routes = jax.vmap(lambda own, number: deal_out(jax.random.fold_in(splits[1], 2), own, number, ROWS_DEV, EXPERTS, TOP, CAP, 2))(routes_keys, routes_turns).reshape((TOKENS, TOP))
    scores = jnp.clip(jnp.exp(math.log(1.0) - 2.9957323 * jax.random.uniform(splits[2], (TOKENS, TOP), jnp.float32) ** shard_levels(splits[2], (TOKENS, TOP), ((0, 128),), -0.2, 0.2)), 0.05, 1.0)
    w_gate = centred(splits[3], (EXPERTS, D, FF), D ** -0.5, 0.09375, ((0, 64), (2, 2)))
    w_up = centred(splits[4], (EXPERTS, D, FF), D ** -0.5, 0.09375, ((0, 64), (2, 2)))
    w_down = centred(splits[5], (EXPERTS, FF, D), FF ** -0.5, 0.15625, ((0, 64), (1, 2)))
    return dict(hidden_in=hidden_in, routes=routes, scores=scores, w_gate=w_gate, w_up=w_up, w_down=w_down)


def reference(hidden_in, routes, scores, w_gate, w_up, w_down):
    values = hidden_in.astype(jnp.float32)
    normed = (values * lax.rsqrt(lax.optimization_barrier(jnp.mean(values * values, -1, keepdims=True)) + 1e-06)).astype(jnp.bfloat16)
    shares = scores / lax.optimization_barrier(jnp.sum(scores, -1, keepdims=True))
    most_rows = N_SEC * N_DEV * CAP
    highest = lax.Precision.HIGHEST

    def per_expert(summed, expert):
        matches = routes == expert
        weight = lax.optimization_barrier(jnp.sum(jnp.where(matches, shares, jnp.float32(0.0)), -1))
        used = jnp.any(matches, -1)
        indices = jnp.nonzero(used, size=most_rows, fill_value=0)[0].astype(jnp.int32)
        taken = normed[indices].astype(jnp.float32)
        gate_part = jnp.dot(taken, w_gate[expert].astype(jnp.float32), precision=highest)
        up_part = jnp.dot(taken, w_up[expert].astype(jnp.float32), precision=highest)
        hidden_part = (jax.nn.silu(gate_part) * up_part).astype(jnp.bfloat16)
        hidden_part = lax.optimization_barrier(hidden_part).astype(jnp.float32)
        output = jnp.dot(hidden_part, w_down[expert].astype(jnp.float32), precision=highest).astype(jnp.bfloat16)
        output = lax.optimization_barrier(output).astype(jnp.float32)
        live_rows = jnp.arange(most_rows, dtype=jnp.int32) < jnp.sum(used.astype(jnp.int32))
        contrib = jnp.where(live_rows[:, None], output * weight[indices][:, None], jnp.float32(0.0))
        return (summed.at[indices].add(contrib), None)
    start_sum = jnp.zeros(hidden_in.shape, jnp.float32)
    summed, _ = lax.scan(per_expert, start_sum, jnp.arange(EXPERTS, dtype=jnp.int32))
    return summed.astype(jnp.bfloat16)
```

```python
import jax
import jax.numpy as jnp
from jax import lax
from jax.experimental import pallas as pl
from jax.experimental.pallas import tpu as pltpu
from jax.sharding import PartitionSpec as P

MESH = pl.DeviceIdType.MESH
BF = jnp.bfloat16
F32 = jnp.float32

ROWS = 32
WIDTH = 4096
HALF = WIDTH // 2
CAP = 8
SLOTS = 2 * CAP
TOK = 2 * ROWS
INFO = 128
SHARE = 64
PARTS = (
    (0, 640, (0, 1, 2)),
    (640, 640, (1, 2, 0)),
    (1280, 768, (2, 0, 1)),
)
STEPS = (1, 3, 2)


def where_am_i():
    dev = lax.axis_index("dev")
    sec = lax.axis_index("sec")
    core = dev % 2
    z = (dev // 2) % 4
    y = ((dev // 8) % 2) * 2 + sec
    x = dev // 16
    return (x, y, z), core


def expert_of(x, y, z, core):
    return ((x * 2 + y // 2) * 4 + z) * 2 + core


def device(pos, core):
    x, y, z = pos
    return {"sec": y % 2, "dev": expert_of(x, y, z, core)}


def moved(pos, axis, to):
    return tuple(to if i == axis else v for i, v in enumerate(pos))


def greet(pos, core):
    barrier = pltpu.get_barrier_semaphore()
    count = 1
    pl.semaphore_signal(barrier, inc=1, device_id=device(pos, 1 - core), device_id_type=MESH)
    for axis in range(3):
        for o in STEPS:
            for c in range(2):
                to = device(moved(pos, axis, (pos[axis] + o) % 4), (core + c) % 2)
                pl.semaphore_signal(barrier, inc=1, device_id=to, device_id_type=MESH)
                count += 1
    pl.semaphore_wait(barrier, count)


def remote(src, dst, send, recv, to):
    return pltpu.make_async_remote_copy(
        src_ref=src, dst_ref=dst, send_sem=send, recv_sem=recv, device_id=to, device_id_type=MESH
    )


def line_expert(pos, axis, d):
    place, core = d // 2, d % 2
    x, y, z = moved(pos, axis, place)
    return expert_of(x, y, z, core)


def at_abc(ref, axes, a, b, lanes):
    index = [None] * 3
    index[axes[0]], index[axes[1]], index[axes[2]] = a, b, slice(None)
    return ref.at[index[0], index[1], index[2], :, lanes]


def lanes_of(p, core):
    first, size, _ = PARTS[p]
    return pl.ds(pl.multiple_of(core * HALF + first, 128), size)


def dispatch_kernel(
    hidden, routes, scores, xexp, i0, i1, i2,
    normed, mine, g0, g1, g2, y0, y1, y2,
    xs, xr, s1, r1, s2, r2, s3, r3, loc,
):
    pos, core = where_am_i()
    gs, ys, infos = (g0, g1, g2), (y0, y1, y2), (i0, i1, i2)
    greet(pos, core)

    values = hidden[...].astype(F32)
    scale = lax.rsqrt(jnp.mean(values * values, -1, keepdims=True) + 1e-06)
    normed[...] = (values * scale).astype(BF)
    share = scores[...] / jnp.sum(scores[...], -1, keepdims=True)
    chosen = routes[...]
    lane = lax.broadcasted_iota(jnp.int32, (ROWS, INFO), 1)
    used = jnp.zeros((ROWS, INFO), F32)
    shares = jnp.zeros((ROWS, INFO), F32)
    for k in range(chosen.shape[1]):
        e = chosen[:, k : k + 1]
        used = used + jnp.where(lane == e, 1.0, 0.0)
        shares = shares + jnp.where(lane == e + SHARE, share[:, k : k + 1], 0.0)
    below = (
        lax.broadcasted_iota(jnp.int32, (ROWS, ROWS), 1)
        < lax.broadcasted_iota(jnp.int32, (ROWS, ROWS), 0)
    ).astype(BF)
    place = jnp.dot(below, used.astype(BF), preferred_element_type=F32)
    mine[...] = jnp.where(lane < SHARE, used * (place + 1.0), shares).astype(BF)

    rows = pl.ds(pl.multiple_of(core * ROWS, ROWS), ROWS)
    partner = device(pos, 1 - core)
    swaps = []
    for p, (first, size, (A, B, C)) in enumerate(PARTS):
        own = gs[p].at[pos[B], pos[C], rows]
        other = remote(
            normed.at[:, lanes_of(p, 1 - core)], own.at[:, :size], xs.at[p, 0], xr.at[p, 0], partner
        )
        extra = remote(mine, own.at[:, size:], xs.at[p, 1], xr.at[p, 1], partner)
        other.start()
        extra.start()
        swaps += [(other, extra)]
        own[:, :size] = normed[:, lanes_of(p, core)]
        own[:, size:] = mine[...]
    first_copies, second_copies, third_copies, kept = {}, {}, {}, {}
    for p, (first, size, (A, B, C)) in enumerate(PARTS):
        for copy in swaps[p]:
            copy.wait_recv()
        for o in STEPS:
            block = gs[p].at[pos[B], pos[C]]
            copy = remote(
                block, block, s1.at[p, o], r1.at[p, o],
                device(moved(pos, C, (pos[C] + o) % 4), core),
            )
            copy.start()
            first_copies[p, o] = copy
    for p, (first, size, (A, B, C)) in enumerate(PARTS):
        for o in STEPS:
            first_copies[p, o].wait_recv()
        for o in STEPS:
            block = gs[p].at[pos[B]]
            copy = remote(
                block, block, s2.at[p, o], r2.at[p, o],
                device(moved(pos, B, (pos[B] + o) % 4), core),
            )
            copy.start()
            second_copies[p, o] = copy

    column = lax.broadcasted_iota(jnp.int32, (8 * 64, INFO), 1)
    drow = lax.broadcasted_iota(jnp.int32, (8 * 64, 1), 0)
    slot = drow % SLOTS
    chip = (drow % 64) // SLOTS
    source = lax.broadcasted_iota(jnp.int32, (1, 4 * TOK), 1)
    fits = (chip == source // TOK) & (slot // CAP == (source // ROWS) % 2)
    for j, b in enumerate((0,) + STEPS):
        for p, (first, size, (A, B, C)) in enumerate(PARTS):
            if b:
                second_copies[p, b].wait_recv()
            bsrc = (pos[B] + 4 - b) % 4
            block = gs[p].at[bsrc]
            info = block[:, :, size:].reshape(4 * TOK, INFO)
            pick = (column == line_expert(pos, A, drow // 64)).astype(BF)
            places = lax.dot_general(pick, info, (((1,), (1,)), ((), ())), preferred_element_type=F32)
            hot = (fits & (places == (slot % CAP + 1).astype(F32))).astype(BF)
            out = jnp.dot(
                hot, block[:, :, :size].reshape(4 * TOK, size), preferred_element_type=F32
            ).astype(BF)
            ys[p][j] = out.reshape(8, 4, SLOTS, size)
            for o in (2, 1, 3, 0):
                a = (pos[A] + o) % 4
                for c in range(2):
                    block_out = ys[p].at[j, 2 * a + (core + c) % 2]
                    target = at_abc(xexp, (A, B, C), pos[A], bsrc, lanes_of(p, core))
                    if o == 0 and c == 0:
                        copy = pltpu.make_async_copy(block_out, target, loc.at[p, j])
                        kept[p, j] = copy
                    else:
                        copy = remote(
                            block_out, target, s3.at[p, j, 2 * o + c], r3.at[p, j, 2 * o + c],
                            device(moved(pos, A, a), (core + c) % 2),
                        )
                        third_copies[p, j, o, c] = copy
                    copy.start()
    for p, (first, size, (A, B, C)) in enumerate(PARTS):
        infos[p][...] = gs[p][:, :, :, size:]
    for copy in kept.values():
        copy.wait()
    for copy in third_copies.values():
        copy.wait()
    for copies in (first_copies, second_copies):
        for copy in copies.values():
            copy.wait_send()
    for pair in swaps:
        for copy in pair:
            copy.wait_send()


def combine_kernel(
    eout, i0, i1, i2, out,
    q0, q1, q2, z0, z1, z2, t0, t1, t2, u0, u1, u2, v0, v1, v2, w, fin,
    s1, r1, s2, r2, s3, r3, loc, xs, xr,
):
    pos, core = where_am_i()
    infos = (i0, i1, i2)
    qs, zs, ts, us, vs = (q0, q1, q2), (z0, z1, z2), (t0, t1, t2), (u0, u1, u2), (v0, v1, v2)
    greet(pos, core)
    first_copies, second_copies, third_copies, kept = {}, {}, {}, {}
    order = (2, 1, 3, 0)
    for b in order:
        for p, (first, size, (A, B, C)) in enumerate(PARTS):
            bto = (pos[B] + b) % 4
            for o in (2, 1, 3, 0):
                a = (pos[A] + o) % 4
                for c in range(2):
                    source = at_abc(eout, (A, B, C), a, bto, lanes_of(p, (core + c) % 2))
                    target = qs[p].at[bto, 2 * pos[A] + core]
                    if o == 0 and c == 0:
                        copy = pltpu.make_async_copy(source, target, loc.at[p, b])
                        kept[p, b] = copy
                    else:
                        copy = remote(
                            source, target, s1.at[p, b, 2 * o + c], r1.at[p, b, 2 * o + c],
                            device(moved(pos, A, a), (core + c) % 2),
                        )
                        first_copies[p, b, o, c] = copy
                    copy.start()

    entry = lax.broadcasted_iota(jnp.int32, (INFO, 8 * 64), 0)
    dcol = lax.broadcasted_iota(jnp.int32, (1, 8 * 64), 1)
    slot = dcol % SLOTS
    chip = (dcol % 64) // SLOTS
    token = lax.broadcasted_iota(jnp.int32, (4 * TOK, 1), 0)
    fits = (chip == token // TOK) & (slot // CAP == (token // ROWS) % 2)
    for b in order:
        for p, (first, size, (A, B, C)) in enumerate(PARTS):
            bto = (pos[B] + b) % 4
            kept[p, b].wait()
            for o in range(4):
                for c in range(2):
                    if o or c:
                        first_copies[p, b, o, c].wait_recv()
            info = infos[p][bto].reshape(4 * TOK, INFO)
            expert = line_expert(pos, A, dcol // 64)
            places = jnp.dot(info, (entry == expert).astype(BF), preferred_element_type=F32)
            shares = jnp.dot(info, (entry == expert + SHARE).astype(BF), preferred_element_type=F32)
            hot = jnp.where(fits & (places == (slot % CAP + 1).astype(F32)), shares, 0.0).astype(BF)
            block = jnp.dot(
                hot, qs[p][bto].reshape(8 * 64, size), preferred_element_type=F32
            ).astype(BF)
            zs[p][bto] = block.reshape(4, TOK, size)
            if b:
                copy = remote(
                    zs[p].at[bto], ts[p].at[b], s2.at[p, b], r2.at[p, b],
                    device(moved(pos, B, bto), core),
                )
                copy.start()
                second_copies[p, b] = copy
    for p, (first, size, (A, B, C)) in enumerate(PARTS):
        total = zs[p][pos[B]].astype(F32)
        for o in STEPS:
            second_copies[p, o].wait_recv()
            total = total + ts[p][o].astype(F32)
        us[p][...] = total.astype(BF)
        for o in STEPS:
            cto = (pos[C] + o) % 4
            copy = remote(
                us[p].at[cto], vs[p].at[o], s3.at[p, o], r3.at[p, o],
                device(moved(pos, C, cto), core),
            )
            copy.start()
            third_copies[p, o] = copy
    partner = device(pos, 1 - core)
    swaps = []
    for p, (first, size, (A, B, C)) in enumerate(PARTS):
        total = us[p][pos[C]].astype(F32)
        for o in STEPS:
            third_copies[p, o].wait_recv()
            total = total + vs[p][o].astype(F32)
        w[:, first : first + size] = total.astype(BF)
        copy = remote(
            w.at[pl.ds(pl.multiple_of((1 - core) * ROWS, ROWS), ROWS), first : first + size],
            fin.at[:, lanes_of(p, core)], xs.at[p], xr.at[p], partner,
        )
        copy.start()
        swaps.append(copy)
    fin[:, pl.ds(pl.multiple_of(core * HALF, 128), HALF)] = w[
        pl.ds(pl.multiple_of(core * ROWS, ROWS), ROWS), :
    ]
    for copy in swaps:
        copy.wait()
    out[...] = fin[...]
    for copies in (first_copies, second_copies, third_copies):
        for copy in copies.values():
            copy.wait_send()


def vmem(*shape):
    return pltpu.VMEM(shape, BF)


def dma(*shape):
    return pltpu.SemaphoreType.DMA(shape)


def on_device(hidden_in, routes, scores, w_gate, w_up, w_down):
    sizes = [size for _, size, _ in PARTS]
    whole = pl.BlockSpec(memory_space=pltpu.VMEM)
    anywhere = pl.BlockSpec(memory_space=pl.ANY)
    xexp, i0, i1, i2 = pl.pallas_call(
        dispatch_kernel,
        out_shape=[jax.ShapeDtypeStruct((4, 4, 4, SLOTS, WIDTH), BF)]
        + [jax.ShapeDtypeStruct((4, 4, TOK, INFO), BF)] * 3,
        in_specs=[whole] * 3,
        out_specs=[anywhere] + [whole] * 3,
        scratch_shapes=[vmem(ROWS, WIDTH), vmem(ROWS, INFO)]
        + [vmem(4, 4, TOK, size + INFO) for size in sizes]
        + [vmem(4, 8, 4, SLOTS, size) for size in sizes]
        + [dma(3, 2), dma(3, 2), dma(3, 4), dma(3, 4), dma(3, 4), dma(3, 4)]
        + [dma(3, 4, 8), dma(3, 4, 8), dma(3, 4)],
        compiler_params=pltpu.CompilerParams(
            collective_id=0, has_side_effects=True, vmem_limit_bytes=48 * 1024 * 1024
        ),
        name="dispatch",
    )(hidden_in, routes, scores)
    rows = xexp.reshape(64 * SLOTS, WIDTH)
    gate_part = jnp.dot(rows, w_gate[0], preferred_element_type=F32)
    up_part = jnp.dot(rows, w_up[0], preferred_element_type=F32)
    hidden_part = (jax.nn.silu(gate_part) * up_part).astype(BF)
    result = jnp.dot(hidden_part, w_down[0], preferred_element_type=F32).astype(BF)
    return pl.pallas_call(
        combine_kernel,
        out_shape=jax.ShapeDtypeStruct((ROWS, WIDTH), BF),
        in_specs=[anywhere] + [whole] * 3,
        out_specs=whole,
        scratch_shapes=[vmem(4, 8, 4, SLOTS, size) for size in sizes]
        + [vmem(4, 4, TOK, size) for size in sizes] * 2
        + [vmem(4, TOK, size) for size in sizes] * 2
        + [vmem(TOK, HALF), vmem(ROWS, WIDTH)]
        + [dma(3, 4, 8), dma(3, 4, 8), dma(3, 4), dma(3, 4), dma(3, 4), dma(3, 4), dma(3, 4)]
        + [dma(3), dma(3)],
        compiler_params=pltpu.CompilerParams(
            collective_id=1, has_side_effects=True, vmem_limit_bytes=48 * 1024 * 1024
        ),
        name="combine",
    )(result.reshape(4, 4, 4, SLOTS, WIDTH), i0, i1, i2)


def solution(mesh):
    placed = (
        P(("sec", "dev"), None),
        P(("sec", "dev"), None),
        P(("sec", "dev"), None),
        P("dev", None, "sec"),
        P("dev", None, "sec"),
        P("dev", "sec", None),
    )
    return jax.shard_map(
        on_device, mesh=mesh, in_specs=placed, out_specs=P(("sec", "dev"), None), check_vma=False
    )
```

```python
import jax
import jax.numpy as jnp
from jax import lax
from jax.experimental import pallas as pl
from jax.experimental.pallas import tpu as pltpu
from jax.sharding import PartitionSpec as P

MESH = pl.DeviceIdType.MESH
BF = jnp.bfloat16
F32 = jnp.float32

ROWS = 32
WIDTH = 4096
HALF = WIDTH // 2
HIDDEN = 768
CAP = 8
SLOTS = 2 * CAP
TOK = 2 * ROWS
INFO = 128
SHARE = 64
AXES = ((0, 1, 2), (1, 2, 0), (2, 0, 1))
PARTS = ((0, 640), (640, 640), (1280, 768))
BACK = ((0, 768), (768, 640), (1408, 640))
STEPS = (1, 3, 2)
ORDER = (2, 1, 3, 0)


def where_am_i():
    dev = lax.axis_index("dev")
    sec = lax.axis_index("sec")
    core = dev % 2
    z = (dev // 2) % 4
    y = ((dev // 8) % 2) * 2 + sec
    x = dev // 16
    return (x, y, z), core


def expert_of(x, y, z, core):
    return ((x * 2 + y // 2) * 4 + z) * 2 + core


def device(pos, core):
    x, y, z = pos
    return {"sec": y % 2, "dev": expert_of(x, y, z, core)}


def moved(pos, axis, to):
    return tuple(to if i == axis else v for i, v in enumerate(pos))


def greet(pos, core):
    barrier = pltpu.get_barrier_semaphore()
    count = 1
    pl.semaphore_signal(barrier, inc=1, device_id=device(pos, 1 - core), device_id_type=MESH)
    for axis in range(3):
        for o in STEPS:
            for c in range(2):
                to = device(moved(pos, axis, (pos[axis] + o) % 4), (core + c) % 2)
                pl.semaphore_signal(barrier, inc=1, device_id=to, device_id_type=MESH)
                count += 1
    pl.semaphore_wait(barrier, count)


def remote(src, dst, send, recv, to):
    return pltpu.make_async_remote_copy(
        src_ref=src, dst_ref=dst, send_sem=send, recv_sem=recv, device_id=to, device_id_type=MESH
    )


def take(ref, sem):
    pltpu.make_async_copy(ref, ref, sem).wait()


def line_expert(pos, axis, d):
    place, core = d // 2, d % 2
    x, y, z = moved(pos, axis, place)
    return expert_of(x, y, z, core)


def half_rows(ref, h, axes, a, b, low, lanes):
    A, B, C = axes
    high, bit = [None] * 3, [None] * 3
    for axis, v in ((A, a), (B, b)):
        high[axis], bit[axis] = v // 2, v % 2
    high[C], bit[C] = slice(None), low
    return ref.at[h, high[0], bit[0], high[1], bit[1], high[2], :, lanes]


def lanes_of(part, core):
    first, size = part
    return pl.ds(pl.multiple_of(core * HALF + first, 128), size)


def kernel(
    hidden, routes, scores, w_gate, w_up, w_down, out,
    hid, rt, sc, gate, up, down, normed, mine,
    g0, g1, g2, y0, y1, y2, xexp, act,
    q0, q1, q2, t0, t1, t2, u0, u1, u2, v0, v1, v2, w, fin,
    ld, xs, xr, s1, r1, s2, r2, s3, r3, loc, bs1, br1, bloc, bs2, br2, bs3, br3, fs, fr,
):
    pos, core = where_am_i()
    gs, ys, qs = (g0, g1, g2), (y0, y1, y2), (q0, q1, q2)
    ts, us, vs = (t0, t1, t2), (u0, u1, u2), (v0, v1, v2)
    loads = [
        pltpu.make_async_copy(src, dst, ld.at[i])
        for i, (src, dst) in enumerate(
            (
                (hidden, hid), (routes, rt), (scores, sc),
                (w_gate.at[0], gate), (w_up.at[0], up), (w_down.at[0], down),
            )
        )
    ]
    for copy in loads[:3]:
        copy.start()
    greet(pos, core)
    for copy in loads[:3]:
        copy.wait()
    for copy in loads[3:]:
        copy.start()

    values = hid[...].astype(F32)
    scale = lax.rsqrt(jnp.mean(values * values, -1, keepdims=True) + 1e-06)
    normed[...] = (values * scale).astype(BF)
    share = sc[...] / jnp.sum(sc[...], 0, keepdims=True)
    chosen = rt[...]
    entry = lax.broadcasted_iota(jnp.int32, (INFO, ROWS), 0)
    used = jnp.zeros((INFO, ROWS), F32)
    shares = jnp.zeros((INFO, ROWS), F32)
    for k in range(chosen.shape[0]):
        e = chosen[k : k + 1]
        used = used + jnp.where(entry == e, 1.0, 0.0)
        shares = shares + jnp.where(entry == e + SHARE, share[k : k + 1], 0.0)
    ahead = lax.broadcasted_iota(jnp.int32, (ROWS, ROWS), 0)
    behind = lax.broadcasted_iota(jnp.int32, (ROWS, ROWS), 1)
    place = jnp.dot(
        used.astype(BF), (ahead < behind).astype(F32).astype(BF), preferred_element_type=F32
    )
    table = jnp.where(entry < SHARE, used * (place + 1.0), shares).astype(BF)
    mine[...] = lax.dot_general(
        (ahead == behind).astype(F32).astype(BF), table, (((1,), (1,)), ((), ())),
        preferred_element_type=F32,
    ).astype(BF)

    rows = pl.ds(pl.multiple_of(core * ROWS, ROWS), ROWS)
    partner = device(pos, 1 - core)
    swaps, first_copies, second_copies = [], {}, {}
    for p, (A, B, C) in enumerate(AXES):
        size = PARTS[p][1]
        own = gs[p].at[pos[B], pos[C] % 2, pos[C] // 2, rows]
        other = remote(
            normed.at[:, lanes_of(PARTS[p], 1 - core)], own.at[:, :size],
            xs.at[p, 0], xr.at[p, 0], partner,
        )
        extra = remote(mine, own.at[:, size:], xs.at[p, 1], xr.at[p, 1], partner)
        other.start()
        extra.start()
        swaps += [(other, extra)]
        own[:, :size] = normed[:, lanes_of(PARTS[p], core)]
        own[:, size:] = mine[...]
    for p, (A, B, C) in enumerate(AXES):
        for copy in swaps[p]:
            copy.wait_recv()
        for o in STEPS:
            block = gs[p].at[pos[B], pos[C] % 2, pos[C] // 2]
            copy = remote(
                block, block, s1.at[p, o], r1.at[p, o],
                device(moved(pos, C, (pos[C] + o) % 4), core),
            )
            copy.start()
            first_copies[p, o] = copy
    for p, (A, B, C) in enumerate(AXES):
        for o in STEPS:
            first_copies[p, o].wait_recv()
        for h in range(2):
            for o in STEPS:
                block = gs[p].at[pos[B], (h + pos[A] + pos[B]) % 2]
                copy = remote(
                    block, block, s2.at[p, h, o], r2.at[p, h, o],
                    device(moved(pos, B, (pos[B] + o) % 4), core),
                )
                copy.start()
                second_copies[p, h, o] = copy

    column = lax.broadcasted_iota(jnp.int32, (8 * 32, INFO), 1)
    drow = lax.broadcasted_iota(jnp.int32, (8 * 32, 1), 0)
    slot = drow % SLOTS
    source = lax.broadcasted_iota(jnp.int32, (1, 2 * TOK), 1)
    fits = ((drow % 32) // SLOTS == source // TOK) & (slot // CAP == (source // ROWS) % 2)
    wanted = (slot % CAP + 1).astype(F32)
    kept = {}
    for h in range(2):
        for j, b in enumerate((0,) + STEPS):
            for p, (A, B, C) in enumerate(AXES):
                size = PARTS[p][1]
                if b:
                    second_copies[p, h, b].wait_recv()
                bsrc = (pos[B] + 4 - b) % 4
                low = (h + pos[A] + bsrc) % 2
                block = gs[p].at[bsrc, low]
                info = block[:, :, size:].reshape(2 * TOK, INFO)
                pick = (column == line_expert(pos, A, drow // 32)).astype(F32).astype(BF)
                places = lax.dot_general(
                    pick, info, (((1,), (1,)), ((), ())), preferred_element_type=F32
                )
                hot = jnp.where(fits & (places == wanted), 1.0, 0.0).astype(BF)
                picked = jnp.dot(
                    hot, block[:, :, :size].reshape(2 * TOK, size), preferred_element_type=F32
                ).astype(BF)
                ys[p][h, j] = picked.reshape(8, 2, SLOTS, size)
                for o in ORDER:
                    a = (pos[A] + o) % 4
                    for c in range(2):
                        sent = ys[p].at[h, j, 2 * a + (core + c) % 2]
                        target = half_rows(
                            xexp, h, (A, B, C), pos[A], bsrc, low, lanes_of(PARTS[p], core)
                        )
                        if o == 0 and c == 0:
                            copy = pltpu.make_async_copy(sent, target, loc.at[p, h, j])
                            kept[p, h, j] = copy
                        else:
                            copy = remote(
                                sent, target, s3.at[p, h, j], r3.at[p, h, j],
                                device(moved(pos, A, a), (core + c) % 2),
                            )
                        copy.start()
    for pair in swaps:
        for copy in pair:
            copy.wait_send()
    for copies in (first_copies, second_copies):
        for copy in copies.values():
            copy.wait_send()

    back_kept = {}
    for h in range(2):
        for j in range(4):
            for p in range(3):
                kept[p, h, j].wait()
                take(ys[p].at[h, j, 0:7], r3.at[p, h, j])
        if h == 0:
            for copy in loads[3:]:
                copy.wait()

        @pl.loop(0, HIDDEN // 256)
        def _(n):
            cols = pl.ds(pl.multiple_of(n * 256, 256), 256)
            taken = xexp[h].reshape(512, WIDTH)
            gate_part = jnp.dot(taken, gate[:, cols], preferred_element_type=F32)
            up_part = jnp.dot(taken, up[:, cols], preferred_element_type=F32)
            act[:, cols] = (gate_part / (1.0 + jnp.exp(-gate_part)) * up_part).astype(BF)

        for c in (1, 0):
            for p, (A, B, C) in enumerate(AXES):
                lanes = lanes_of(BACK[p], (core + c) % 2)
                result = jnp.dot(act[...], down[:, lanes], preferred_element_type=F32).astype(BF)
                xexp[h, :, :, :, :, :, :, lanes] = result.reshape(
                    2, 2, 2, 2, 2, SLOTS, BACK[p][1]
                )
                for b in ORDER:
                    bto = (pos[B] + b) % 4
                    for o in ORDER:
                        a = (pos[A] + o) % 4
                        sent = half_rows(xexp, h, (A, B, C), a, bto, (h + a + bto) % 2, lanes)
                        target = qs[p].at[h, bto, 2 * pos[A] + core]
                        if o == 0 and c == 0:
                            copy = pltpu.make_async_copy(sent, target, bloc.at[p, h, b])
                            back_kept[p, h, b] = copy
                        else:
                            copy = remote(
                                sent, target, bs1.at[p, h, b], br1.at[p, h, b],
                                device(moved(pos, A, a), (core + c) % 2),
                            )
                        copy.start()

    entry = lax.broadcasted_iota(jnp.int32, (INFO, 8 * 32), 0)
    dcol = lax.broadcasted_iota(jnp.int32, (1, 8 * 32), 1)
    slot = dcol % SLOTS
    token = lax.broadcasted_iota(jnp.int32, (2 * TOK, 1), 0)
    fits = ((dcol % 32) // SLOTS == token // TOK) & (slot // CAP == (token // ROWS) % 2)
    wanted = (slot % CAP + 1).astype(F32)
    second_back, third_back = {}, {}
    for h in range(2):
        for b in ORDER:
            for p, (A, B, C) in enumerate(AXES):
                size, back = PARTS[p][1], BACK[p][1]
                bto = (pos[B] + b) % 4
                low = (h + pos[A] + bto) % 2
                back_kept[p, h, b].wait()
                take(qs[p].at[h, bto, 0:7], br1.at[p, h, b])
                info = gs[p].at[bto, low][:, :, size:].reshape(2 * TOK, INFO)
                expert = line_expert(pos, A, dcol // 32)
                places = jnp.dot(
                    info, (entry == expert).astype(F32).astype(BF), preferred_element_type=F32
                )
                weights = jnp.dot(
                    info, (entry == expert + SHARE).astype(F32).astype(BF),
                    preferred_element_type=F32,
                )
                hot = jnp.where(fits & (places == wanted), weights, 0.0).astype(BF)
                block = jnp.dot(
                    hot, qs[p][h, bto].reshape(8 * 32, back), preferred_element_type=F32
                ).astype(BF)
                if b:
                    ts[p][0, h, b] = block.reshape(2, TOK, back)
                    copy = remote(
                        ts[p].at[0, h, b], ts[p].at[1, h, b], bs2.at[p, h, b], br2.at[p, h, b],
                        device(moved(pos, B, bto), core),
                    )
                    copy.start()
                    second_back[p, h, b] = copy
                else:
                    ts[p][0, h, 0] = block.reshape(2, TOK, back)
    for h in range(2):
        for p, (A, B, C) in enumerate(AXES):
            total = ts[p][0, h, 0].astype(F32)
            for o in STEPS:
                second_back[p, h, o].wait_recv()
                total = total + ts[p][1, h, o].astype(F32)
            us[p][(h + pos[A] + pos[B]) % 2] = total.astype(BF)
    for p, (A, B, C) in enumerate(AXES):
        for o in STEPS:
            cto = (pos[C] + o) % 4
            copy = remote(
                us[p].at[cto % 2, cto // 2], vs[p].at[o], bs3.at[p, o], br3.at[p, o],
                device(moved(pos, C, cto), core),
            )
            copy.start()
            third_back[p, o] = copy
    finals = []
    for p, (A, B, C) in enumerate(AXES):
        first, back = BACK[p]
        total = us[p][pos[C] % 2, pos[C] // 2].astype(F32)
        for o in STEPS:
            third_back[p, o].wait_recv()
            total = total + vs[p][o].astype(F32)
        w[:, first : first + back] = total.astype(BF)
        copy = remote(
            w.at[pl.ds(pl.multiple_of((1 - core) * ROWS, ROWS), ROWS), first : first + back],
            fin.at[:, lanes_of(BACK[p], core)], fs.at[p], fr.at[p], partner,
        )
        copy.start()
        finals.append(copy)
    fin[:, pl.ds(pl.multiple_of(core * HALF, 128), HALF)] = w[rows, :]
    for copy in finals:
        copy.wait()
    out[...] = fin[...]
    for h in range(2):
        for p in range(3):
            for j in range(4):
                take(ys[p].at[h, j, 0:7], s3.at[p, h, j])
                take(qs[p].at[h, j, 0:7], bs1.at[p, h, j])
    for copies in (second_back, third_back):
        for copy in copies.values():
            copy.wait_send()


def vmem(*shape):
    return pltpu.VMEM(shape, BF)


def dma(*shape):
    return pltpu.SemaphoreType.DMA(shape)


def on_device(hidden_in, routes, scores, w_gate, w_up, w_down):
    sizes = [size for _, size in PARTS]
    backs = [size for _, size in BACK]
    top = routes.shape[1]
    anywhere = pl.BlockSpec(memory_space=pl.ANY)
    return pl.pallas_call(
        kernel,
        out_shape=jax.ShapeDtypeStruct((ROWS, WIDTH), BF),
        in_specs=[anywhere] * 6,
        out_specs=pl.BlockSpec(memory_space=pltpu.VMEM),
        scratch_shapes=[vmem(ROWS, WIDTH)]
        + [pltpu.VMEM((top, ROWS), jnp.int32), pltpu.VMEM((top, ROWS), F32)]
        + [vmem(WIDTH, HIDDEN), vmem(WIDTH, HIDDEN), vmem(HIDDEN, WIDTH)]
        + [vmem(ROWS, WIDTH), vmem(ROWS, INFO)]
        + [vmem(4, 2, 2, TOK, size + INFO) for size in sizes]
        + [vmem(2, 4, 8, 2, SLOTS, size) for size in sizes]
        + [vmem(2, 2, 2, 2, 2, 2, SLOTS, WIDTH), vmem(512, HIDDEN)]
        + [vmem(2, 4, 8, 2, SLOTS, size) for size in backs]
        + [vmem(2, 2, 4, 2, TOK, size) for size in backs]
        + [vmem(2, 2, TOK, size) for size in backs]
        + [vmem(4, TOK, size) for size in backs]
        + [vmem(TOK, HALF), vmem(ROWS, WIDTH)]
        + [dma(6), dma(3, 2), dma(3, 2), dma(3, 4), dma(3, 4), dma(3, 2, 4), dma(3, 2, 4)]
        + [dma(3, 2, 4)] * 6
        + [dma(3, 2, 4), dma(3, 2, 4), dma(3, 4), dma(3, 4), dma(3), dma(3)],
        compiler_params=pltpu.CompilerParams(
            collective_id=0, has_side_effects=True, vmem_limit_bytes=67_000_000
        ),
        name="experts",
    )(hidden_in, routes.T, scores.T, w_gate, w_up, w_down)


def solution(mesh):
    placed = (
        P(("sec", "dev"), None),
        P(("sec", "dev"), None),
        P(("sec", "dev"), None),
        P("dev", None, "sec"),
        P("dev", None, "sec"),
        P("dev", "sec", None),
    )
    return jax.shard_map(
        on_device, mesh=mesh, in_specs=placed, out_specs=P(("sec", "dev"), None), check_vma=False
    )
```

```python
import jax
import jax.numpy as jnp
from jax import lax
from jax.experimental import pallas as pl
from jax.experimental.pallas import tpu as pltpu
from jax.sharding import PartitionSpec as P

MESH = pl.DeviceIdType.MESH
BF = jnp.bfloat16
F32 = jnp.float32

ROWS = 32
WIDTH = 4096
HALF = WIDTH // 2
HIDDEN = 768
CAP = 8
SLOTS = 2 * CAP
TOK = 2 * ROWS
INFO = 128
SHARE = 64
AXES = ((0, 1, 2), (1, 2, 0), (2, 0, 1))
PARTS = ((0, 640), (640, 640), (1280, 768))
BACK = ((0, 768), (768, 640), (1408, 640))
STEPS = (1, 3, 2)
ORDER = (2, 1, 3, 0)


def where_am_i():
    dev = lax.axis_index("dev")
    sec = lax.axis_index("sec")
    core = dev % 2
    z = (dev // 2) % 4
    y = ((dev // 8) % 2) * 2 + sec
    x = dev // 16
    return (x, y, z), core


def expert_of(x, y, z, core):
    return ((x * 2 + y // 2) * 4 + z) * 2 + core


def device(pos, core):
    x, y, z = pos
    return {"sec": y % 2, "dev": expert_of(x, y, z, core)}


def moved(pos, axis, to):
    return tuple(to if i == axis else v for i, v in enumerate(pos))


def greet(pos, core):
    barrier = pltpu.get_barrier_semaphore()
    count = 1
    pl.semaphore_signal(barrier, inc=1, device_id=device(pos, 1 - core), device_id_type=MESH)
    for axis in range(3):
        for o in STEPS:
            for c in range(2):
                to = device(moved(pos, axis, (pos[axis] + o) % 4), (core + c) % 2)
                pl.semaphore_signal(barrier, inc=1, device_id=to, device_id_type=MESH)
                count += 1
    return count


def remote(src, dst, send, recv, to):
    return pltpu.make_async_remote_copy(
        src_ref=src, dst_ref=dst, send_sem=send, recv_sem=recv, device_id=to, device_id_type=MESH
    )


def take(ref, sem):
    pltpu.make_async_copy(ref, ref, sem).wait()


def line_expert(pos, axis, d):
    place, core = d // 2, d % 2
    x, y, z = moved(pos, axis, place)
    return expert_of(x, y, z, core)


def half_rows(ref, h, axes, a, b, low, lanes):
    A, B, C = axes
    high, bit = [None] * 3, [None] * 3
    for axis, v in ((A, a), (B, b)):
        high[axis], bit[axis] = v // 2, v % 2
    high[C], bit[C] = slice(None), low
    return ref.at[h, high[0], bit[0], high[1], bit[1], high[2], :, lanes]


def lanes_of(part, core):
    first, size = part
    return pl.ds(pl.multiple_of(core * HALF + first, 128), size)


def kernel(
    hidden, routes, scores, w_gate, w_up, w_down, out,
    hid, rt, sc, gate, up, down, m0, m1, m2,
    g0, g1, g2, y0, y1, y2, xexp, act,
    q0, q1, q2, t0, t1, t2, u0, u1, u2, v0, v1, v2,
    ld, s1, r1, s2, r2, f2, e2, s3, r3, loc, bs1, br1, bloc, bs2, br2, bs3, br3,
):
    pos, core = where_am_i()
    ms, gs, ys, qs = (m0, m1, m2), (g0, g1, g2), (y0, y1, y2), (q0, q1, q2)
    ts, us, vs = (t0, t1, t2), (u0, u1, u2), (v0, v1, v2)
    loads = [
        pltpu.make_async_copy(src, dst, ld.at[i])
        for i, (src, dst) in enumerate(
            (
                (hidden, hid), (routes, rt), (scores, sc),
                (w_gate.at[0], gate), (w_up.at[0], up), (w_down.at[0], down),
            )
        )
    ]
    for copy in loads[:3]:
        copy.start()
    peers = greet(pos, core)
    for copy in loads[:3]:
        copy.wait()
    for copy in loads[3:]:
        copy.start()

    share = sc[...] / jnp.sum(sc[...], 0, keepdims=True)
    chosen = rt[...]
    entry = lax.broadcasted_iota(jnp.int32, (INFO, ROWS), 0)
    used = jnp.zeros((INFO, ROWS), F32)
    shares = jnp.zeros((INFO, ROWS), F32)
    for k in range(chosen.shape[0]):
        e = chosen[k : k + 1]
        used = used + jnp.where(entry == e, 1.0, 0.0)
        shares = shares + jnp.where(entry == e + SHARE, share[k : k + 1], 0.0)
    ahead = lax.broadcasted_iota(jnp.int32, (ROWS, ROWS), 0)
    behind = lax.broadcasted_iota(jnp.int32, (ROWS, ROWS), 1)
    place = jnp.dot(
        used.astype(BF), (ahead < behind).astype(F32).astype(BF), preferred_element_type=F32
    )
    table = jnp.where(entry < SHARE, used * (place + 1.0), shares).astype(BF)
    mine = lax.dot_general(
        (ahead == behind).astype(F32).astype(BF), table, (((1,), (1,)), ((), ())),
        preferred_element_type=F32,
    ).astype(BF)
    values = hid[...].astype(F32)
    scale = lax.rsqrt(jnp.mean(values * values, -1, keepdims=True) + 1e-06)
    normed = (values * scale).astype(BF)
    for p, (first, size) in enumerate(PARTS):
        for c in range(2):
            ms[p][c, :, :size] = normed[:, c * HALF + first : c * HALF + first + size]
            ms[p][c, :, size:] = mine
    pl.semaphore_wait(pltpu.get_barrier_semaphore(), peers)

    rows = pl.ds(pl.multiple_of(core * ROWS, ROWS), ROWS)
    first_copies, second_copies, forwards = {}, {}, {}
    for p, (A, B, C) in enumerate(AXES):
        own = gs[p].at[pos[B], pos[C] % 2, pos[C] // 2, rows]
        for o in (2, 1, 3, 0):
            for c in range(2):
                if o or c:
                    copy = remote(
                        ms[p].at[(core + c) % 2], own, s1.at[p, o, c], r1.at[p, o, c],
                        device(moved(pos, C, (pos[C] + o) % 4), (core + c) % 2),
                    )
                    copy.start()
                    first_copies[p, o, c] = copy
        own[...] = ms[p][core]
    for p, (A, B, C) in enumerate(AXES):
        for o in range(4):
            for c in range(2):
                if o or c:
                    first_copies[p, o, c].wait_recv()
        for h in range(2):
            for o in (1, 3):
                block = gs[p].at[pos[B], (h + pos[A] + pos[B]) % 2]
                copy = remote(
                    block, block, s2.at[p, h, o], r2.at[p, h, o],
                    device(moved(pos, B, (pos[B] + o) % 4), core),
                )
                copy.start()
                second_copies[p, h, o] = copy

    def forward(h):
        for p, (A, B, C) in enumerate(AXES):
            for o in (1, 3):
                second_copies[p, h, o].wait_recv()
                bsrc = (pos[B] + 4 - o) % 4
                piece = gs[p].at[bsrc, (h + pos[A] + bsrc) % 2, o // 2]
                copy = remote(
                    piece, piece, f2.at[p, h, o], e2.at[p, h, o],
                    device(moved(pos, B, (pos[B] + o) % 4), core),
                )
                copy.start()
                forwards[p, h, o] = copy

    column = lax.broadcasted_iota(jnp.int32, (8 * 32, INFO), 1)
    drow = lax.broadcasted_iota(jnp.int32, (8 * 32, 1), 0)
    slot = drow % SLOTS
    source = lax.broadcasted_iota(jnp.int32, (1, 2 * TOK), 1)
    fits = ((drow % 32) // SLOTS == source // TOK) & (slot // CAP == (source // ROWS) % 2)
    wanted = (slot % CAP + 1).astype(F32)
    kept = {}
    for h in range(2):
        for j, b in enumerate((0,) + STEPS):
            if j == 1:
                forward(h)
            for p, (A, B, C) in enumerate(AXES):
                size = PARTS[p][1]
                if b == 2:
                    for o in (1, 3):
                        forwards[p, h, o].wait_recv()
                bsrc = (pos[B] + 4 - b) % 4
                low = (h + pos[A] + bsrc) % 2
                block = gs[p].at[bsrc, low]
                info = block[:, :, size:].reshape(2 * TOK, INFO)
                pick = (column == line_expert(pos, A, drow // 32)).astype(F32).astype(BF)
                places = lax.dot_general(
                    pick, info, (((1,), (1,)), ((), ())), preferred_element_type=F32
                )
                hot = jnp.where(fits & (places == wanted), 1.0, 0.0).astype(BF)
                picked = jnp.dot(
                    hot, block[:, :, :size].reshape(2 * TOK, size), preferred_element_type=F32
                ).astype(BF)
                ys[p][h, j] = picked.reshape(8, 2, SLOTS, size)
                for o in ORDER:
                    a = (pos[A] + o) % 4
                    for c in range(2):
                        sent = ys[p].at[h, j, 2 * a + (core + c) % 2]
                        target = half_rows(
                            xexp, h, (A, B, C), pos[A], bsrc, low, lanes_of(PARTS[p], core)
                        )
                        if o == 0 and c == 0:
                            copy = pltpu.make_async_copy(sent, target, loc.at[p, h, j])
                            kept[p, h, j] = copy
                        else:
                            copy = remote(
                                sent, target, s3.at[p, h, j], r3.at[p, h, j],
                                device(moved(pos, A, a), (core + c) % 2),
                            )
                        copy.start()
    for copies in (first_copies, second_copies, forwards):
        for copy in copies.values():
            copy.wait_send()

    back_kept = {}
    for h in range(2):
        for j in range(4):
            for p in range(3):
                kept[p, h, j].wait()
                take(ys[p].at[h, j, 0:7], r3.at[p, h, j])
        if h == 0:
            for copy in loads[3:]:
                copy.wait()

        @pl.loop(0, HIDDEN // 256)
        def _(n):
            cols = pl.ds(pl.multiple_of(n * 256, 256), 256)
            taken = xexp[h].reshape(512, WIDTH)
            gate_part = jnp.dot(taken, gate[:, cols], preferred_element_type=F32)
            up_part = jnp.dot(taken, up[:, cols], preferred_element_type=F32)
            act[:, cols] = (gate_part / (1.0 + jnp.exp(-gate_part)) * up_part).astype(BF)

        for p, (A, B, C) in enumerate(AXES):
            for c in (1, 0):
                lanes = lanes_of(BACK[p], (core + c) % 2)
                result = jnp.dot(act[...], down[:, lanes], preferred_element_type=F32).astype(BF)
                xexp[h, :, :, :, :, :, :, lanes] = result.reshape(
                    2, 2, 2, 2, 2, SLOTS, BACK[p][1]
                )
            for b in ORDER:
                bto = (pos[B] + b) % 4
                for o in ORDER:
                    a = (pos[A] + o) % 4
                    for c in (1, 0):
                        lanes = lanes_of(BACK[p], (core + c) % 2)
                        sent = half_rows(xexp, h, (A, B, C), a, bto, (h + a + bto) % 2, lanes)
                        target = qs[p].at[h, bto, 2 * pos[A] + core]
                        if o == 0 and c == 0:
                            copy = pltpu.make_async_copy(sent, target, bloc.at[p, h, b])
                            back_kept[p, h, b] = copy
                        else:
                            copy = remote(
                                sent, target, bs1.at[p, h, b], br1.at[p, h, b],
                                device(moved(pos, A, a), (core + c) % 2),
                            )
                        copy.start()

    entry = lax.broadcasted_iota(jnp.int32, (INFO, 8 * 32), 0)
    dcol = lax.broadcasted_iota(jnp.int32, (1, 8 * 32), 1)
    slot = dcol % SLOTS
    token = lax.broadcasted_iota(jnp.int32, (2 * TOK, 1), 0)
    fits = ((dcol % 32) // SLOTS == token // TOK) & (slot // CAP == (token // ROWS) % 2)
    wanted = (slot % CAP + 1).astype(F32)
    second_back, third_back = {}, {}
    for h in range(2):
        for b in ORDER:
            for p, (A, B, C) in enumerate(AXES):
                size, back = PARTS[p][1], BACK[p][1]
                bto = (pos[B] + b) % 4
                low = (h + pos[A] + bto) % 2
                back_kept[p, h, b].wait()
                take(qs[p].at[h, bto, 0:7], br1.at[p, h, b])
                info = gs[p].at[bto, low][:, :, size:].reshape(2 * TOK, INFO)
                expert = line_expert(pos, A, dcol // 32)
                places = jnp.dot(
                    info, (entry == expert).astype(F32).astype(BF), preferred_element_type=F32
                )
                weights = jnp.dot(
                    info, (entry == expert + SHARE).astype(F32).astype(BF),
                    preferred_element_type=F32,
                )
                hot = jnp.where(fits & (places == wanted), weights, 0.0).astype(BF)
                block = jnp.dot(
                    hot, qs[p][h, bto].reshape(8 * 32, back), preferred_element_type=F32
                ).astype(BF)
                if b:
                    ts[p][0, h, b] = block.reshape(2, TOK, back)
                    copy = remote(
                        ts[p].at[0, h, b], ts[p].at[1, h, b], bs2.at[p, h, b], br2.at[p, h, b],
                        device(moved(pos, B, bto), core),
                    )
                    copy.start()
                    second_back[p, h, b] = copy
                else:
                    ts[p][0, h, 0] = block.reshape(2, TOK, back)
    for h in range(2):
        for p, (A, B, C) in enumerate(AXES):
            total = ts[p][0, h, 0].astype(F32)
            for o in STEPS:
                second_back[p, h, o].wait_recv()
                total = total + ts[p][1, h, o].astype(F32)
            us[p][(h + pos[A] + pos[B]) % 2] = total.astype(BF)
    for p, (A, B, C) in enumerate(AXES):
        for o in ORDER:
            cto = (pos[C] + o) % 4
            for c in range(2):
                if o or c:
                    to = (core + c) % 2
                    copy = remote(
                        us[p].at[cto % 2, cto // 2, pl.ds(pl.multiple_of(to * ROWS, ROWS), ROWS)],
                        vs[p].at[o, c], bs3.at[p, o, c], br3.at[p, o, c],
                        device(moved(pos, C, cto), to),
                    )
                    copy.start()
                    third_back[p, o, c] = copy
    for p, (A, B, C) in enumerate(AXES):
        vs[p][0, 0] = us[p][pos[C] % 2, pos[C] // 2, rows]
        for c in range(2):
            total = jnp.zeros((ROWS, BACK[p][1]), F32)
            for o in range(4):
                if o or c:
                    third_back[p, o, c].wait_recv()
                total = total + vs[p][o, c].astype(F32)
            out[:, lanes_of(BACK[p], (core + c) % 2)] = total.astype(BF)
    for h in range(2):
        for p in range(3):
            for j in range(4):
                take(ys[p].at[h, j, 0:7], s3.at[p, h, j])
                take(qs[p].at[h, j, 0:7], bs1.at[p, h, j])
    for copies in (second_back, third_back):
        for copy in copies.values():
            copy.wait_send()


def vmem(*shape):
    return pltpu.VMEM(shape, BF)


def dma(*shape):
    return pltpu.SemaphoreType.DMA(shape)


def on_device(hidden_in, routes, scores, w_gate, w_up, w_down):
    sizes = [size for _, size in PARTS]
    backs = [size for _, size in BACK]
    top = routes.shape[1]
    anywhere = pl.BlockSpec(memory_space=pl.ANY)
    return pl.pallas_call(
        kernel,
        out_shape=jax.ShapeDtypeStruct((ROWS, WIDTH), BF),
        in_specs=[anywhere] * 6,
        out_specs=pl.BlockSpec(memory_space=pltpu.VMEM),
        scratch_shapes=[vmem(ROWS, WIDTH)]
        + [pltpu.VMEM((top, ROWS), jnp.int32), pltpu.VMEM((top, ROWS), F32)]
        + [vmem(WIDTH, HIDDEN), vmem(WIDTH, HIDDEN), vmem(HIDDEN, WIDTH)]
        + [vmem(2, ROWS, size + INFO) for size in sizes]
        + [vmem(4, 2, 2, TOK, size + INFO) for size in sizes]
        + [vmem(2, 4, 8, 2, SLOTS, size) for size in sizes]
        + [vmem(2, 2, 2, 2, 2, 2, SLOTS, WIDTH), vmem(512, HIDDEN)]
        + [vmem(2, 4, 8, 2, SLOTS, size) for size in backs]
        + [vmem(2, 2, 4, 2, TOK, size) for size in backs]
        + [vmem(2, 2, TOK, size) for size in backs]
        + [vmem(4, 2, ROWS, size) for size in backs]
        + [dma(6), dma(3, 4, 2), dma(3, 4, 2)]
        + [dma(3, 2, 4)] * 12
        + [dma(3, 4, 2), dma(3, 4, 2)],
        compiler_params=pltpu.CompilerParams(
            collective_id=0, has_side_effects=True, vmem_limit_bytes=67_000_000
        ),
        name="experts",
    )(hidden_in, routes.T, scores.T, w_gate, w_up, w_down)


def solution(mesh):
    placed = (
        P(("sec", "dev"), None),
        P(("sec", "dev"), None),
        P(("sec", "dev"), None),
        P("dev", None, "sec"),
        P("dev", None, "sec"),
        P("dev", "sec", None),
    )
    return jax.shard_map(
        on_device, mesh=mesh, in_specs=placed, out_specs=P(("sec", "dev"), None), check_vma=False
    )
```

```python
import jax
import jax.numpy as jnp
from jax import lax
from jax.experimental import pallas as pl
from jax.experimental.pallas import tpu as pltpu
from jax.sharding import PartitionSpec as P

MESH = pl.DeviceIdType.MESH
BF = jnp.bfloat16
F32 = jnp.float32

ROWS = 32
WIDTH = 4096
HALF = WIDTH // 2
HIDDEN = 768
CAP = 8
SLOTS = 2 * CAP
TOK = 2 * ROWS
INFO = 128
SHARE = 64
AXES = ((0, 1, 2), (1, 2, 0), (2, 0, 1))
PARTS = ((0, 640), (640, 640), (1280, 768))
BACK = ((0, 768), (768, 640), (1408, 640))
STEPS = (1, 3, 2)
ORDER = (2, 1, 3, 0)


def where_am_i():
    dev = lax.axis_index("dev")
    sec = lax.axis_index("sec")
    core = dev % 2
    z = (dev // 2) % 4
    y = ((dev // 8) % 2) * 2 + sec
    x = dev // 16
    return (x, y, z), core


def expert_of(x, y, z, core):
    return ((x * 2 + y // 2) * 4 + z) * 2 + core


def device(pos, core):
    x, y, z = pos
    return {"sec": y % 2, "dev": expert_of(x, y, z, core)}


def moved(pos, axis, to):
    return tuple(to if i == axis else v for i, v in enumerate(pos))


def greet(pos, core):
    barrier = pltpu.get_barrier_semaphore()
    count = 1
    pl.semaphore_signal(barrier, inc=1, device_id=device(pos, 1 - core), device_id_type=MESH)
    for axis in range(3):
        for o in STEPS:
            for c in range(2):
                to = device(moved(pos, axis, (pos[axis] + o) % 4), (core + c) % 2)
                pl.semaphore_signal(barrier, inc=1, device_id=to, device_id_type=MESH)
                count += 1
    return count


def remote(src, dst, send, recv, to):
    return pltpu.make_async_remote_copy(
        src_ref=src, dst_ref=dst, send_sem=send, recv_sem=recv, device_id=to, device_id_type=MESH
    )


def take(ref, sem):
    pltpu.make_async_copy(ref, ref, sem).wait()


def line_expert(pos, axis, d):
    place, core = d // 2, d % 2
    x, y, z = moved(pos, axis, place)
    return expert_of(x, y, z, core)


def half_rows(ref, h, axes, a, b, low, lanes):
    A, B, C = axes
    high, bit = [None] * 3, [None] * 3
    for axis, v in ((A, a), (B, b)):
        high[axis], bit[axis] = v // 2, v % 2
    high[C], bit[C] = slice(None), low
    return ref.at[h, high[0], bit[0], high[1], bit[1], high[2], :, lanes]


def lanes_of(part, core):
    first, size = part
    return pl.ds(pl.multiple_of(core * HALF + first, 128), size)


def kernel(
    hidden, routes, scores, w_gate, w_up, w_down, out,
    hid, rt, sc, gate, up, down, m0, m1, m2,
    g0, g1, g2, y0, y1, y2, xexp, act,
    q0, q1, q2, t0, t1, t2, u0, u1, u2, v0, v1, v2,
    ld, s1, r1, s2, r2, f2, e2, s3, r3, loc, bs1, br1, bloc, bs2, br2, bs3, br3,
):
    pos, core = where_am_i()
    ms, gs, ys, qs = (m0, m1, m2), (g0, g1, g2), (y0, y1, y2), (q0, q1, q2)
    ts, us, vs = (t0, t1, t2), (u0, u1, u2), (v0, v1, v2)
    loads = [
        pltpu.make_async_copy(src, dst, ld.at[i])
        for i, (src, dst) in enumerate(
            (
                (hidden, hid), (routes, rt), (scores, sc),
                (w_gate.at[0], gate), (w_up.at[0], up), (w_down.at[0], down),
            )
        )
    ]
    for copy in loads[:3]:
        copy.start()
    peers = greet(pos, core)
    for copy in loads[:3]:
        copy.wait()
    for copy in loads[3:]:
        copy.start()

    share = sc[...] / jnp.sum(sc[...], 0, keepdims=True)
    chosen = rt[...]
    entry = lax.broadcasted_iota(jnp.int32, (INFO, ROWS), 0)
    used = jnp.zeros((INFO, ROWS), F32)
    shares = jnp.zeros((INFO, ROWS), F32)
    for k in range(chosen.shape[0]):
        e = chosen[k : k + 1]
        used = used + jnp.where(entry == e, 1.0, 0.0)
        shares = shares + jnp.where(entry == e + SHARE, share[k : k + 1], 0.0)
    ahead = lax.broadcasted_iota(jnp.int32, (ROWS, ROWS), 0)
    behind = lax.broadcasted_iota(jnp.int32, (ROWS, ROWS), 1)
    place = jnp.dot(
        used.astype(BF), (ahead < behind).astype(F32).astype(BF), preferred_element_type=F32
    )
    table = jnp.where(entry < SHARE, used * (place + 1.0), shares).astype(BF)
    mine = lax.dot_general(
        (ahead == behind).astype(F32).astype(BF), table, (((1,), (1,)), ((), ())),
        preferred_element_type=F32,
    ).astype(BF)
    values = hid[...].astype(F32)
    scale = lax.rsqrt(jnp.mean(values * values, -1, keepdims=True) + 1e-06)
    normed = (values * scale).astype(BF)
    for p, (first, size) in enumerate(PARTS):
        for c in range(2):
            ms[p][c, :, :size] = normed[:, c * HALF + first : c * HALF + first + size]
            ms[p][c, :, size:] = mine
    pl.semaphore_wait(pltpu.get_barrier_semaphore(), peers)

    rows = pl.ds(pl.multiple_of(core * ROWS, ROWS), ROWS)
    first_copies, second_copies, forwards = {}, {}, {}
    for p, (A, B, C) in enumerate(AXES):
        own = gs[p].at[pos[B], pos[C] % 2, pos[C] // 2, rows]
        for o in (2, 1, 3, 0):
            for c in range(2):
                if o or c:
                    copy = remote(
                        ms[p].at[(core + c) % 2], own, s1.at[p, o, c], r1.at[p, o, c],
                        device(moved(pos, C, (pos[C] + o) % 4), (core + c) % 2),
                    )
                    copy.start()
                    first_copies[p, o, c] = copy
        own[...] = ms[p][core]
    for p, (A, B, C) in enumerate(AXES):
        for o in range(4):
            for c in range(2):
                if o or c:
                    first_copies[p, o, c].wait_recv()
        for h in range(2):
            for o in (1, 3):
                block = gs[p].at[pos[B], (h + pos[A] + pos[B]) % 2]
                copy = remote(
                    block, block, s2.at[p, h, o], r2.at[p, h, o],
                    device(moved(pos, B, (pos[B] + o) % 4), core),
                )
                copy.start()
                second_copies[p, h, o] = copy

    def forward(h):
        for p, (A, B, C) in enumerate(AXES):
            for o in (1, 3):
                second_copies[p, h, o].wait_recv()
                bsrc = (pos[B] + 4 - o) % 4
                piece = gs[p].at[bsrc, (h + pos[A] + bsrc) % 2, o // 2]
                copy = remote(
                    piece, piece, f2.at[p, h, o], e2.at[p, h, o],
                    device(moved(pos, B, (pos[B] + o) % 4), core),
                )
                copy.start()
                forwards[p, h, o] = copy

    column = lax.broadcasted_iota(jnp.int32, (8 * 32, INFO), 1)
    drow = lax.broadcasted_iota(jnp.int32, (8 * 32, 1), 0)
    slot = drow % SLOTS
    source = lax.broadcasted_iota(jnp.int32, (1, 2 * TOK), 1)
    fits = ((drow % 32) // SLOTS == source // TOK) & (slot // CAP == (source // ROWS) % 2)
    wanted = (slot % CAP + 1).astype(F32)
    kept = {}
    for h in range(2):
        for j, b in enumerate((0,) + STEPS):
            if j == 1:
                forward(h)
            for p, (A, B, C) in enumerate(AXES):
                size = PARTS[p][1]
                if b == 2:
                    for o in (1, 3):
                        forwards[p, h, o].wait_recv()
                bsrc = (pos[B] + 4 - b) % 4
                low = (h + pos[A] + bsrc) % 2
                block = gs[p].at[bsrc, low]
                info = block[:, :, size:].reshape(2 * TOK, INFO)
                pick = (column == line_expert(pos, A, drow // 32)).astype(F32).astype(BF)
                places = lax.dot_general(
                    pick, info, (((1,), (1,)), ((), ())), preferred_element_type=F32
                )
                hot = jnp.where(fits & (places == wanted), 1.0, 0.0).astype(BF)
                picked = jnp.dot(
                    hot, block[:, :, :size].reshape(2 * TOK, size), preferred_element_type=F32
                ).astype(BF)
                ys[p][h, j] = picked.reshape(8, 2, SLOTS, size)
                for o in ORDER:
                    a = (pos[A] + o) % 4
                    for c in range(2):
                        sent = ys[p].at[h, j, 2 * a + (core + c) % 2]
                        target = half_rows(
                            xexp, h, (A, B, C), pos[A], bsrc, low, lanes_of(PARTS[p], core)
                        )
                        if o == 0 and c == 0:
                            copy = pltpu.make_async_copy(sent, target, loc.at[p, h, j])
                            kept[p, h, j] = copy
                        else:
                            copy = remote(
                                sent, target, s3.at[p, h, j], r3.at[p, h, j],
                                device(moved(pos, A, a), (core + c) % 2),
                            )
                        copy.start()
    for copies in (first_copies, second_copies, forwards):
        for copy in copies.values():
            copy.wait_send()

    back_kept = {}
    for h in range(2):
        for j in range(4):
            for p in range(3):
                kept[p, h, j].wait()
                take(ys[p].at[h, j, 0:7], r3.at[p, h, j])
        if h == 0:
            for copy in loads[3:]:
                copy.wait()

        @pl.loop(0, HIDDEN // 256)
        def _(n):
            cols = pl.ds(pl.multiple_of(n * 256, 256), 256)
            taken = xexp[h].reshape(512, WIDTH)
            gate_part = jnp.dot(taken, gate[:, cols], preferred_element_type=F32)
            up_part = jnp.dot(taken, up[:, cols], preferred_element_type=F32)
            act[:, cols] = (gate_part / (1.0 + jnp.exp(-gate_part)) * up_part).astype(BF)

        for p, (A, B, C) in enumerate(AXES):
            for c in (1, 0):
                lanes = lanes_of(BACK[p], (core + c) % 2)
                result = jnp.dot(act[...], down[:, lanes], preferred_element_type=F32).astype(BF)
                xexp[h, :, :, :, :, :, :, lanes] = result.reshape(
                    2, 2, 2, 2, 2, SLOTS, BACK[p][1]
                )
            for b in ORDER:
                bto = (pos[B] + b) % 4
                for o in ORDER:
                    a = (pos[A] + o) % 4
                    for c in (1, 0):
                        lanes = lanes_of(BACK[p], (core + c) % 2)
                        sent = half_rows(xexp, h, (A, B, C), a, bto, (h + a + bto) % 2, lanes)
                        target = qs[p].at[h, bto, 2 * pos[A] + core]
                        if o == 0 and c == 0:
                            copy = pltpu.make_async_copy(sent, target, bloc.at[p, h, b])
                            back_kept[p, h, b] = copy
                        else:
                            copy = remote(
                                sent, target, bs1.at[p, h, b], br1.at[p, h, b],
                                device(moved(pos, A, a), (core + c) % 2),
                            )
                        copy.start()

    entry = lax.broadcasted_iota(jnp.int32, (INFO, 8 * 32), 0)
    dcol = lax.broadcasted_iota(jnp.int32, (1, 8 * 32), 1)
    slot = dcol % SLOTS
    token = lax.broadcasted_iota(jnp.int32, (2 * TOK, 1), 0)
    fits = ((dcol % 32) // SLOTS == token // TOK) & (slot // CAP == (token // ROWS) % 2)
    wanted = (slot % CAP + 1).astype(F32)
    second_back = {}
    for h in range(2):
        for b in ORDER:
            for p, (A, B, C) in enumerate(AXES):
                size, back = PARTS[p][1], BACK[p][1]
                bto = (pos[B] + b) % 4
                low = (h + pos[A] + bto) % 2
                back_kept[p, h, b].wait()
                take(qs[p].at[h, bto, 0:7], br1.at[p, h, b])
                info = gs[p].at[bto, low][:, :, size:].reshape(2 * TOK, INFO)
                expert = line_expert(pos, A, dcol // 32)
                places = jnp.dot(
                    info, (entry == expert).astype(F32).astype(BF), preferred_element_type=F32
                )
                weights = jnp.dot(
                    info, (entry == expert + SHARE).astype(F32).astype(BF),
                    preferred_element_type=F32,
                )
                hot = jnp.where(fits & (places == wanted), weights, 0.0).astype(BF)
                block = jnp.dot(
                    hot, qs[p][h, bto].reshape(8 * 32, back), preferred_element_type=F32
                ).astype(BF)
                if b:
                    ts[p][0, h, b] = block.reshape(2, TOK, back)
                    copy = remote(
                        ts[p].at[0, h, b], ts[p].at[1, h, b], bs2.at[p, h, b], br2.at[p, h, b],
                        device(moved(pos, B, bto), core),
                    )
                    copy.start()
                    second_back[p, h, b] = copy
                else:
                    ts[p][0, h, 0] = block.reshape(2, TOK, back)
    for h in range(2):
        for p, (A, B, C) in enumerate(AXES):
            total = ts[p][0, h, 0].astype(F32)
            for o in STEPS:
                second_back[p, h, o].wait_recv()
                total = total + ts[p][1, h, o].astype(F32)
            low = (h + pos[A] + pos[B]) % 2
            us[p][low] = total.astype(BF)
            for high in range(2):
                cto = 2 * high + low
                o = (cto + 4 - pos[C]) % 4
                for c in (1, 0):
                    to = (core + c) % 2
                    copy = remote(
                        us[p].at[low, high, pl.ds(pl.multiple_of(to * ROWS, ROWS), ROWS)],
                        vs[p].at[o, c], bs3.at[p, o, c], br3.at[p, o, c],
                        device(moved(pos, C, cto), to),
                    )
                    if c:
                        copy.start()
                    else:
                        pl.when(o != 0)(copy.start)
    for p, (A, B, C) in enumerate(AXES):
        vs[p][0, 0] = us[p][pos[C] % 2, pos[C] // 2, rows]
        for c in range(2):
            total = jnp.zeros((ROWS, BACK[p][1]), F32)
            for o in range(4):
                if o or c:
                    take(vs[p].at[o, c], br3.at[p, o, c])
                total = total + vs[p][o, c].astype(F32)
            out[:, lanes_of(BACK[p], (core + c) % 2)] = total.astype(BF)
    for p in range(3):
        for o in range(4):
            for c in range(2):
                if o or c:
                    take(vs[p].at[o, c], bs3.at[p, o, c])
    for h in range(2):
        for p in range(3):
            for j in range(4):
                take(ys[p].at[h, j, 0:7], s3.at[p, h, j])
                take(qs[p].at[h, j, 0:7], bs1.at[p, h, j])
    for copy in second_back.values():
        copy.wait_send()


def vmem(*shape):
    return pltpu.VMEM(shape, BF)


def dma(*shape):
    return pltpu.SemaphoreType.DMA(shape)


def on_device(hidden_in, routes, scores, w_gate, w_up, w_down):
    sizes = [size for _, size in PARTS]
    backs = [size for _, size in BACK]
    top = routes.shape[1]
    anywhere = pl.BlockSpec(memory_space=pl.ANY)
    return pl.pallas_call(
        kernel,
        out_shape=pltpu.VMEM((ROWS, WIDTH), BF),
        in_specs=[anywhere] * 6,
        out_specs=pl.BlockSpec(memory_space=pltpu.VMEM),
        scratch_shapes=[vmem(ROWS, WIDTH)]
        + [pltpu.VMEM((top, ROWS), jnp.int32), pltpu.VMEM((top, ROWS), F32)]
        + [vmem(WIDTH, HIDDEN), vmem(WIDTH, HIDDEN), vmem(HIDDEN, WIDTH)]
        + [vmem(2, ROWS, size + INFO) for size in sizes]
        + [vmem(4, 2, 2, TOK, size + INFO) for size in sizes]
        + [vmem(2, 4, 8, 2, SLOTS, size) for size in sizes]
        + [vmem(2, 2, 2, 2, 2, 2, SLOTS, WIDTH), vmem(512, HIDDEN)]
        + [vmem(2, 4, 8, 2, SLOTS, size) for size in backs]
        + [vmem(2, 2, 4, 2, TOK, size) for size in backs]
        + [vmem(2, 2, TOK, size) for size in backs]
        + [vmem(4, 2, ROWS, size) for size in backs]
        + [dma(6), dma(3, 4, 2), dma(3, 4, 2)]
        + [dma(3, 2, 4)] * 12
        + [dma(3, 4, 2), dma(3, 4, 2)],
        compiler_params=pltpu.CompilerParams(
            collective_id=0, has_side_effects=True, vmem_limit_bytes=62_500_000
        ),
        name="experts",
    )(hidden_in, routes.T, scores.T, w_gate, w_up, w_down)


def solution(mesh):
    placed = (
        P(("sec", "dev"), None),
        P(("sec", "dev"), None),
        P(("sec", "dev"), None),
        P("dev", None, "sec"),
        P("dev", None, "sec"),
        P("dev", "sec", None),
    )
    return jax.shard_map(
        on_device, mesh=mesh, in_specs=placed, out_specs=P(("sec", "dev"), None), check_vma=False
    )
```

```python
import jax
import jax.numpy as jnp
from jax import lax
from jax.experimental import pallas as pl
from jax.experimental.pallas import tpu as pltpu
from jax.sharding import PartitionSpec as P

MESH = pl.DeviceIdType.MESH
BF = jnp.bfloat16
F32 = jnp.float32

ROWS = 32
WIDTH = 4096
HALF = WIDTH // 2
HIDDEN = 768
CAP = 8
SLOTS = 2 * CAP
TOK = 2 * ROWS
INFO = 128
SHARE = 64
AXES = ((0, 1, 2), (1, 2, 0), (2, 0, 1))
PARTS = ((0, 640), (640, 640), (1280, 768))
BACK = ((0, 768), (768, 640), (1408, 640))
STEPS = (1, 3, 2)
ORDER = (2, 1, 3, 0)


def where_am_i():
    dev = lax.axis_index("dev")
    sec = lax.axis_index("sec")
    core = dev % 2
    z = (dev // 2) % 4
    y = ((dev // 8) % 2) * 2 + sec
    x = dev // 16
    return (x, y, z), core


def expert_of(x, y, z, core):
    return ((x * 2 + y // 2) * 4 + z) * 2 + core


def device(pos, core):
    x, y, z = pos
    return {"sec": y % 2, "dev": expert_of(x, y, z, core)}


def moved(pos, axis, to):
    return tuple(to if i == axis else v for i, v in enumerate(pos))


def greet(pos, core):
    barrier = pltpu.get_barrier_semaphore()
    count = 1
    pl.semaphore_signal(barrier, inc=1, device_id=device(pos, 1 - core), device_id_type=MESH)
    for axis in range(3):
        for o in STEPS:
            for c in range(2):
                to = device(moved(pos, axis, (pos[axis] + o) % 4), (core + c) % 2)
                pl.semaphore_signal(barrier, inc=1, device_id=to, device_id_type=MESH)
                count += 1
    return count


def remote(src, dst, send, recv, to):
    return pltpu.make_async_remote_copy(
        src_ref=src, dst_ref=dst, send_sem=send, recv_sem=recv, device_id=to, device_id_type=MESH
    )


def take(ref, sem):
    pltpu.make_async_copy(ref, ref, sem).wait()


def line_expert(pos, axis, d):
    place, core = d // 2, d % 2
    x, y, z = moved(pos, axis, place)
    return expert_of(x, y, z, core)


def half_rows(ref, h, axes, a, b, low, lanes):
    A, B, C = axes
    high, bit = [None] * 3, [None] * 3
    for axis, v in ((A, a), (B, b)):
        high[axis], bit[axis] = v // 2, v % 2
    high[C], bit[C] = slice(None), low
    return ref.at[h, high[0], bit[0], high[1], bit[1], high[2], :, lanes]


def lanes_of(part, core):
    first, size = part
    return pl.ds(pl.multiple_of(core * HALF + first, 128), size)


def kernel(
    hidden, routes, scores, w_gate, w_up, w_down, out,
    hid, rt, sc, gate, up, down, m0, m1, m2,
    g0, g1, g2, y0, y1, y2, xexp, act,
    q0, q1, q2, t0, t1, t2, u0, u1, u2, v0, v1, v2,
    ld, s1, r1, es, s2, r2, f2, e2, s3, r3, loc, bs1, br1, bloc, bs2, br2, bs3, br3,
):
    pos, core = where_am_i()
    ms, gs, ys, qs = (m0, m1, m2), (g0, g1, g2), (y0, y1, y2), (q0, q1, q2)
    ts, us, vs = (t0, t1, t2), (u0, u1, u2), (v0, v1, v2)
    loads = [
        pltpu.make_async_copy(src, dst, ld.at[i])
        for i, (src, dst) in enumerate(
            (
                (hidden, hid), (routes, rt), (scores, sc),
                (w_gate.at[0], gate), (w_up.at[0], up), (w_down.at[0], down),
            )
        )
    ]
    for copy in loads[:3]:
        copy.start()
    peers = greet(pos, core)
    for copy in loads[:3]:
        copy.wait()
    for copy in loads[3:]:
        copy.start()

    share = sc[...] / jnp.sum(sc[...], 0, keepdims=True)
    chosen = rt[...]
    entry = lax.broadcasted_iota(jnp.int32, (INFO, ROWS), 0)
    used = jnp.zeros((INFO, ROWS), F32)
    shares = jnp.zeros((INFO, ROWS), F32)
    for k in range(chosen.shape[0]):
        e = chosen[k : k + 1]
        used = used + jnp.where(entry == e, 1.0, 0.0)
        shares = shares + jnp.where(entry == e + SHARE, share[k : k + 1], 0.0)
    ahead = lax.broadcasted_iota(jnp.int32, (ROWS, ROWS), 0)
    behind = lax.broadcasted_iota(jnp.int32, (ROWS, ROWS), 1)
    place = jnp.dot(
        used.astype(BF), (ahead < behind).astype(F32).astype(BF), preferred_element_type=F32
    )
    table = jnp.where(entry < SHARE, used * (place + 1.0), shares).astype(BF)
    mine = lax.dot_general(
        (ahead == behind).astype(F32).astype(BF), table, (((1,), (1,)), ((), ())),
        preferred_element_type=F32,
    ).astype(BF)
    values = hid[...].astype(F32)
    scale = lax.rsqrt(jnp.mean(values * values, -1, keepdims=True) + 1e-06)
    normed = (values * scale).astype(BF)
    for p, (first, size) in enumerate(PARTS):
        for c in range(2):
            ms[p][c, :, :size] = normed[:, c * HALF + first : c * HALF + first + size]
            ms[p][c, :, size:] = mine
    pl.semaphore_wait(pltpu.get_barrier_semaphore(), peers)

    rows = pl.ds(pl.multiple_of(core * ROWS, ROWS), ROWS)
    first_copies, early, second_copies, forwards = {}, {}, {}, {}
    for p, (A, B, C) in enumerate(AXES):
        own = gs[p].at[pos[B], pos[C] % 2, pos[C] // 2, rows]
        for o in (2, 1, 3, 0):
            for c in range(2):
                if o or c:
                    copy = remote(
                        ms[p].at[(core + c) % 2], own, s1.at[p, o, c], r1.at[p, o, c],
                        device(moved(pos, C, (pos[C] + o) % 4), (core + c) % 2),
                    )
                    copy.start()
                    first_copies[p, o, c] = copy
        own[...] = ms[p][core]
    for p, (A, B, C) in enumerate(AXES):
        own = gs[p].at[pos[B], pos[C] % 2, pos[C] // 2, rows]
        h = (pos[A] + pos[B] + pos[C]) % 2
        for o in (1, 3):
            for c in range(2):
                copy = remote(
                    ms[p].at[(core + c) % 2], own, es.at[p, o, c], r2.at[p, h, o, pos[C] // 2],
                    device(moved(pos, B, (pos[B] + o) % 4), (core + c) % 2),
                )
                copy.start()
                early[p, o, c] = copy
    for p, (A, B, C) in enumerate(AXES):
        for o in range(4):
            for c in range(2):
                if o or c:
                    first_copies[p, o, c].wait_recv()
        for h in range(2):
            low = (h + pos[A] + pos[B]) % 2
            for o in (1, 3):
                for high in range(2):
                    block = gs[p].at[pos[B], low, high]
                    copy = remote(
                        block, block, s2.at[p, h, o, high], r2.at[p, h, o, high],
                        device(moved(pos, B, (pos[B] + o) % 4), core),
                    )
                    rest = 2 * high + low != pos[C]
                    pl.when(rest)(copy.start)
                    second_copies[p, h, o, high] = rest, copy

    def forward(h):
        for p, (A, B, C) in enumerate(AXES):
            for o in (1, 3):
                bsrc = (pos[B] + 4 - o) % 4
                piece = gs[p].at[bsrc, (h + pos[A] + bsrc) % 2, o // 2]
                take(piece, r2.at[p, h, o, o // 2])
                copy = remote(
                    piece, piece, f2.at[p, h, o], e2.at[p, h, o],
                    device(moved(pos, B, (pos[B] + o) % 4), core),
                )
                copy.start()
                forwards[p, h, o] = copy

    column = lax.broadcasted_iota(jnp.int32, (8 * 32, INFO), 1)
    drow = lax.broadcasted_iota(jnp.int32, (8 * 32, 1), 0)
    slot = drow % SLOTS
    source = lax.broadcasted_iota(jnp.int32, (1, 2 * TOK), 1)
    fits = ((drow % 32) // SLOTS == source // TOK) & (slot // CAP == (source // ROWS) % 2)
    wanted = (slot % CAP + 1).astype(F32)
    kept = {}
    for h in range(2):
        for j, b in enumerate((0,) + STEPS):
            if j == 1:
                forward(h)
            for p, (A, B, C) in enumerate(AXES):
                size = PARTS[p][1]
                if b == 2:
                    for o in (1, 3):
                        forwards[p, h, o].wait_recv()
                bsrc = (pos[B] + 4 - b) % 4
                low = (h + pos[A] + bsrc) % 2
                block = gs[p].at[bsrc, low]
                if b in (1, 3):
                    take(block.at[1 - b // 2], r2.at[p, h, b, 1 - b // 2])
                info = block[:, :, size:].reshape(2 * TOK, INFO)
                pick = (column == line_expert(pos, A, drow // 32)).astype(F32).astype(BF)
                places = lax.dot_general(
                    pick, info, (((1,), (1,)), ((), ())), preferred_element_type=F32
                )
                hot = jnp.where(fits & (places == wanted), 1.0, 0.0).astype(BF)
                picked = jnp.dot(
                    hot, block[:, :, :size].reshape(2 * TOK, size), preferred_element_type=F32
                ).astype(BF)
                ys[p][h, j] = picked.reshape(8, 2, SLOTS, size)
                for o in ORDER:
                    a = (pos[A] + o) % 4
                    for c in range(2):
                        sent = ys[p].at[h, j, 2 * a + (core + c) % 2]
                        target = half_rows(
                            xexp, h, (A, B, C), pos[A], bsrc, low, lanes_of(PARTS[p], core)
                        )
                        if o == 0 and c == 0:
                            copy = pltpu.make_async_copy(sent, target, loc.at[p, h, j])
                            kept[p, h, j] = copy
                        else:
                            copy = remote(
                                sent, target, s3.at[p, h, j], r3.at[p, h, j],
                                device(moved(pos, A, a), (core + c) % 2),
                            )
                        copy.start()
    for copies in (first_copies, early, forwards):
        for copy in copies.values():
            copy.wait_send()
    for rest, copy in second_copies.values():
        pl.when(rest)(copy.wait_send)

    back_kept = {}
    for h in range(2):
        for j in range(4):
            for p in range(3):
                kept[p, h, j].wait()
                take(ys[p].at[h, j, 0:7], r3.at[p, h, j])
        if h == 0:
            for copy in loads[3:]:
                copy.wait()

        @pl.loop(0, HIDDEN // 256)
        def _(n):
            cols = pl.ds(pl.multiple_of(n * 256, 256), 256)
            taken = xexp[h].reshape(512, WIDTH)
            gate_part = jnp.dot(taken, gate[:, cols], preferred_element_type=F32)
            up_part = jnp.dot(taken, up[:, cols], preferred_element_type=F32)
            act[:, cols] = (gate_part / (1.0 + jnp.exp(-gate_part)) * up_part).astype(BF)

        for p, (A, B, C) in enumerate(AXES):
            for c in (1, 0):
                lanes = lanes_of(BACK[p], (core + c) % 2)
                result = jnp.dot(act[...], down[:, lanes], preferred_element_type=F32).astype(BF)
                xexp[h, :, :, :, :, :, :, lanes] = result.reshape(
                    2, 2, 2, 2, 2, SLOTS, BACK[p][1]
                )
            for b in ORDER:
                bto = (pos[B] + b) % 4
                for o in ORDER:
                    a = (pos[A] + o) % 4
                    for c in (1, 0):
                        lanes = lanes_of(BACK[p], (core + c) % 2)
                        sent = half_rows(xexp, h, (A, B, C), a, bto, (h + a + bto) % 2, lanes)
                        target = qs[p].at[h, bto, 2 * pos[A] + core]
                        if o == 0 and c == 0:
                            copy = pltpu.make_async_copy(sent, target, bloc.at[p, h, b])
                            back_kept[p, h, b] = copy
                        else:
                            copy = remote(
                                sent, target, bs1.at[p, h, b], br1.at[p, h, b],
                                device(moved(pos, A, a), (core + c) % 2),
                            )
                        copy.start()

    entry = lax.broadcasted_iota(jnp.int32, (INFO, 8 * 32), 0)
    dcol = lax.broadcasted_iota(jnp.int32, (1, 8 * 32), 1)
    slot = dcol % SLOTS
    token = lax.broadcasted_iota(jnp.int32, (2 * TOK, 1), 0)
    fits = ((dcol % 32) // SLOTS == token // TOK) & (slot // CAP == (token // ROWS) % 2)
    wanted = (slot % CAP + 1).astype(F32)
    second_back = {}

    def weigh(h, b, p):
        A, B, C = AXES[p]
        size, back = PARTS[p][1], BACK[p][1]
        bto = (pos[B] + b) % 4
        back_kept[p, h, b].wait()
        take(qs[p].at[h, bto, 0:7], br1.at[p, h, b])
        info = gs[p].at[bto, (h + pos[A] + bto) % 2][:, :, size:].reshape(2 * TOK, INFO)
        expert = line_expert(pos, A, dcol // 32)
        places = jnp.dot(
            info, (entry == expert).astype(F32).astype(BF), preferred_element_type=F32
        )
        weights = jnp.dot(
            info, (entry == expert + SHARE).astype(F32).astype(BF), preferred_element_type=F32
        )
        hot = jnp.where(fits & (places == wanted), weights, 0.0).astype(BF)
        return jnp.dot(hot, qs[p][h, bto].reshape(8 * 32, back), preferred_element_type=F32)

    def pass_on(h, b, p, src, dst, which):
        to = device(moved(pos, AXES[p][1], (pos[AXES[p][1]] + b) % 4), core)
        copy = remote(src, dst, bs2.at[p, h, which], br2.at[p, h, which], to)
        copy.start()
        second_back[p, h, which] = copy

    for p in range(3):
        ts[p][0, 0, 2] = weigh(0, 2, p).astype(BF).reshape(2, TOK, BACK[p][1])
        pass_on(0, 1, p, ts[p].at[0, 0, 2, 0], ts[p].at[1, 0, 2, 0], 2)
        pass_on(0, 3, p, ts[p].at[0, 0, 2, 1], ts[p].at[1, 0, 2, 1], 0)
    for p in range(3):
        ts[p][0, 0, 0] = weigh(0, 0, p).astype(BF).reshape(2, TOK, BACK[p][1])
    for b in ORDER:
        for p in range(3):
            ts[p][0, 1, b] = weigh(1, b, p).astype(BF).reshape(2, TOK, BACK[p][1])
            if b:
                pass_on(1, b, p, ts[p].at[0, 1, b], ts[p].at[1, 1, b], b)
    for b, which in ((1, 2), (3, 0)):
        for p in range(3):
            high = b // 2
            block = weigh(0, b, p).reshape(2, TOK, BACK[p][1])
            second_back[p, 0, which].wait_recv()
            ts[p][0, 0, b, high] = (block[high] + ts[p][1, 0, 2, high].astype(F32)).astype(BF)
            ts[p][0, 0, b, 1 - high] = block[1 - high].astype(BF)
            pass_on(0, b, p, ts[p].at[0, 0, b], ts[p].at[1, 0, b], b)
    for h in (1, 0):
        for p, (A, B, C) in enumerate(AXES):
            total = ts[p][0, h, 0].astype(F32)
            for o in STEPS if h else (1, 3):
                second_back[p, h, o].wait_recv()
                total = total + ts[p][1, h, o].astype(F32)
            low = (h + pos[A] + pos[B]) % 2
            us[p][low] = total.astype(BF)
            for high in range(2):
                cto = 2 * high + low
                o = (cto + 4 - pos[C]) % 4
                for c in (1, 0):
                    to = (core + c) % 2
                    copy = remote(
                        us[p].at[low, high, pl.ds(pl.multiple_of(to * ROWS, ROWS), ROWS)],
                        vs[p].at[o, c], bs3.at[p, o, c], br3.at[p, o, c],
                        device(moved(pos, C, cto), to),
                    )
                    if c:
                        copy.start()
                    else:
                        pl.when(o != 0)(copy.start)
    for p, (A, B, C) in enumerate(AXES):
        vs[p][0, 0] = us[p][pos[C] % 2, pos[C] // 2, rows]
        for c in range(2):
            total = jnp.zeros((ROWS, BACK[p][1]), F32)
            for o in range(4):
                if o or c:
                    take(vs[p].at[o, c], br3.at[p, o, c])
                total = total + vs[p][o, c].astype(F32)
            out[:, lanes_of(BACK[p], (core + c) % 2)] = total.astype(BF)
    for p in range(3):
        for o in range(4):
            for c in range(2):
                if o or c:
                    take(vs[p].at[o, c], bs3.at[p, o, c])
    for h in range(2):
        for p in range(3):
            for j in range(4):
                take(ys[p].at[h, j, 0:7], s3.at[p, h, j])
                take(qs[p].at[h, j, 0:7], bs1.at[p, h, j])
    for copy in second_back.values():
        copy.wait_send()


def vmem(*shape):
    return pltpu.VMEM(shape, BF)


def dma(*shape):
    return pltpu.SemaphoreType.DMA(shape)


def on_device(hidden_in, routes, scores, w_gate, w_up, w_down):
    sizes = [size for _, size in PARTS]
    backs = [size for _, size in BACK]
    top = routes.shape[1]
    anywhere = pl.BlockSpec(memory_space=pl.ANY)
    return pl.pallas_call(
        kernel,
        out_shape=pltpu.VMEM((ROWS, WIDTH), BF),
        in_specs=[anywhere] * 6,
        out_specs=pl.BlockSpec(memory_space=pltpu.VMEM),
        scratch_shapes=[vmem(ROWS, WIDTH)]
        + [pltpu.VMEM((top, ROWS), jnp.int32), pltpu.VMEM((top, ROWS), F32)]
        + [vmem(WIDTH, HIDDEN), vmem(WIDTH, HIDDEN), vmem(HIDDEN, WIDTH)]
        + [vmem(2, ROWS, size + INFO) for size in sizes]
        + [vmem(4, 2, 2, TOK, size + INFO) for size in sizes]
        + [vmem(2, 4, 8, 2, SLOTS, size) for size in sizes]
        + [vmem(2, 2, 2, 2, 2, 2, SLOTS, WIDTH), vmem(512, HIDDEN)]
        + [vmem(2, 4, 8, 2, SLOTS, size) for size in backs]
        + [vmem(2, 2, 4, 2, TOK, size) for size in backs]
        + [vmem(2, 2, TOK, size) for size in backs]
        + [vmem(4, 2, ROWS, size) for size in backs]
        + [dma(6), dma(3, 4, 2), dma(3, 4, 2)]
        + [dma(3, 4, 2), dma(3, 2, 4, 2), dma(3, 2, 4, 2)]
        + [dma(3, 2, 4)] * 10
        + [dma(3, 4, 2), dma(3, 4, 2)],
        compiler_params=pltpu.CompilerParams(
            collective_id=0, has_side_effects=True, vmem_limit_bytes=62_500_000
        ),
        name="experts",
    )(hidden_in, routes.T, scores.T, w_gate, w_up, w_down)


def solution(mesh):
    placed = (
        P(("sec", "dev"), None),
        P(("sec", "dev"), None),
        P(("sec", "dev"), None),
        P("dev", None, "sec"),
        P("dev", None, "sec"),
        P("dev", "sec", None),
    )
    return jax.shard_map(
        on_device, mesh=mesh, in_specs=placed, out_specs=P(("sec", "dev"), None), check_vma=False
    )
```

```python
import jax
import jax.numpy as jnp
from jax import lax
from jax.experimental import pallas as pl
from jax.experimental.pallas import tpu as pltpu
from jax.sharding import PartitionSpec as P

MESH = pl.DeviceIdType.MESH
BF = jnp.bfloat16
F32 = jnp.float32

ROWS = 32
WIDTH = 4096
HALF = WIDTH // 2
HIDDEN = 768
CAP = 8
SLOTS = 2 * CAP
TOK = 2 * ROWS
INFO = 128
SHARE = 64
AXES = ((0, 1, 2), (1, 2, 0), (2, 0, 1))
PARTS = ((0, 640), (640, 640), (1280, 768))
BACK = ((0, 768), (768, 640), (1408, 640))
STEPS = (1, 3, 2)
ORDER = (2, 1, 3, 0)


def where_am_i():
    dev = lax.axis_index("dev")
    sec = lax.axis_index("sec")
    core = dev % 2
    z = (dev // 2) % 4
    y = ((dev // 8) % 2) * 2 + sec
    x = dev // 16
    return (x, y, z), core


def expert_of(x, y, z, core):
    return ((x * 2 + y // 2) * 4 + z) * 2 + core


def device(pos, core):
    x, y, z = pos
    return {"sec": y % 2, "dev": expert_of(x, y, z, core)}


def moved(pos, axis, to):
    return tuple(to if i == axis else v for i, v in enumerate(pos))


def greet(pos, core):
    barrier = pltpu.get_barrier_semaphore()
    count = 1
    pl.semaphore_signal(barrier, inc=1, device_id=device(pos, 1 - core), device_id_type=MESH)
    for axis in range(3):
        for o in STEPS:
            for c in range(2):
                to = device(moved(pos, axis, (pos[axis] + o) % 4), (core + c) % 2)
                pl.semaphore_signal(barrier, inc=1, device_id=to, device_id_type=MESH)
                count += 1
    return count


def remote(src, dst, send, recv, to):
    return pltpu.make_async_remote_copy(
        src_ref=src, dst_ref=dst, send_sem=send, recv_sem=recv, device_id=to, device_id_type=MESH
    )


def take(ref, sem):
    pltpu.make_async_copy(ref, ref, sem).wait()


def line_expert(pos, axis, d):
    place, core = d // 2, d % 2
    x, y, z = moved(pos, axis, place)
    return expert_of(x, y, z, core)


def half_rows(ref, h, axes, a, b, low, lanes):
    A, B, C = axes
    high, bit = [None] * 3, [None] * 3
    for axis, v in ((A, a), (B, b)):
        high[axis], bit[axis] = v // 2, v % 2
    high[C], bit[C] = slice(None), low
    return ref.at[h, high[0], bit[0], high[1], bit[1], high[2], :, lanes]


def lanes_of(part, core):
    first, size = part
    return pl.ds(pl.multiple_of(core * HALF + first, 128), size)


def kernel(
    hidden, routes, scores, w_gate, w_up, w_down, out,
    hid, rt, sc, gate, up, down, m0, m1, m2,
    g0, g1, g2, y0, y1, y2, xexp, act,
    q0, q1, q2, t0, t1, t2, u0, u1, u2, v0, v1, v2,
    ld, s1, r1, es, s2, r2, f2, e2, s3, r3, loc, bs1, br1, bloc, bs2, br2, bs3, br3,
):
    pos, core = where_am_i()
    ms, gs, ys, qs = (m0, m1, m2), (g0, g1, g2), (y0, y1, y2), (q0, q1, q2)
    ts, us, vs = (t0, t1, t2), (u0, u1, u2), (v0, v1, v2)
    loads = [
        pltpu.make_async_copy(src, dst, ld.at[i])
        for i, (src, dst) in enumerate(
            (
                (hidden, hid), (routes, rt), (scores, sc),
                (w_gate.at[0], gate), (w_up.at[0], up), (w_down.at[0], down),
            )
        )
    ]
    for copy in loads[:3]:
        copy.start()
    peers = greet(pos, core)
    for copy in loads[1:3]:
        copy.wait()

    share = sc[...] / jnp.sum(sc[...], 0, keepdims=True)
    chosen = rt[...]
    entry = lax.broadcasted_iota(jnp.int32, (INFO, ROWS), 0)
    used = jnp.zeros((INFO, ROWS), F32)
    shares = jnp.zeros((INFO, ROWS), F32)
    for k in range(chosen.shape[0]):
        e = chosen[k : k + 1]
        used = used + jnp.where(entry == e, 1.0, 0.0)
        shares = shares + jnp.where(entry == e + SHARE, share[k : k + 1], 0.0)
    ahead = lax.broadcasted_iota(jnp.int32, (ROWS, ROWS), 0)
    behind = lax.broadcasted_iota(jnp.int32, (ROWS, ROWS), 1)
    place = jnp.dot(
        used.astype(BF), (ahead < behind).astype(F32).astype(BF), preferred_element_type=F32
    )
    table = jnp.where(entry < SHARE, used * (place + 1.0), shares).astype(BF)
    mine = lax.dot_general(
        (ahead == behind).astype(F32).astype(BF), table, (((1,), (1,)), ((), ())),
        preferred_element_type=F32,
    ).astype(BF)
    loads[0].wait()
    values = hid[...].astype(F32)
    scale = lax.rsqrt(jnp.mean(values * values, -1, keepdims=True) + 1e-06)
    normed = (values * scale).astype(BF)
    for p, (first, size) in enumerate(PARTS):
        for c in range(2):
            ms[p][c, :, :size] = normed[:, c * HALF + first : c * HALF + first + size]
            ms[p][c, :, size:] = mine
    pl.semaphore_wait(pltpu.get_barrier_semaphore(), peers)

    rows = pl.ds(pl.multiple_of(core * ROWS, ROWS), ROWS)
    first_copies, early, second_copies, forwards = {}, {}, {}, {}
    for p, (A, B, C) in enumerate(AXES):
        own = gs[p].at[pos[B], pos[C] % 2, pos[C] // 2, rows]
        for o in (2, 1, 3, 0):
            for c in range(2):
                if o or c:
                    copy = remote(
                        ms[p].at[(core + c) % 2], own, s1.at[p, o, c], r1.at[p, o, c],
                        device(moved(pos, C, (pos[C] + o) % 4), (core + c) % 2),
                    )
                    copy.start()
                    first_copies[p, o, c] = copy
        own[...] = ms[p][core]
    for p, (A, B, C) in enumerate(AXES):
        own = gs[p].at[pos[B], pos[C] % 2, pos[C] // 2, rows]
        h = (pos[A] + pos[B] + pos[C]) % 2
        for o in (1, 3):
            for c in range(2):
                copy = remote(
                    ms[p].at[(core + c) % 2], own, es.at[p, o, c], r2.at[p, h, o, pos[C] // 2],
                    device(moved(pos, B, (pos[B] + o) % 4), (core + c) % 2),
                )
                copy.start()
                early[p, o, c] = copy
    for p, (A, B, C) in enumerate(AXES):
        for o in range(4):
            for c in range(2):
                if o or c:
                    first_copies[p, o, c].wait_recv()
        for h in range(2):
            low = (h + pos[A] + pos[B]) % 2
            for o in (1, 3):
                for high in range(2):
                    block = gs[p].at[pos[B], low, high]
                    copy = remote(
                        block, block, s2.at[p, h, o, high], r2.at[p, h, o, high],
                        device(moved(pos, B, (pos[B] + o) % 4), core),
                    )
                    rest = 2 * high + low != pos[C]
                    pl.when(rest)(copy.start)
                    second_copies[p, h, o, high] = rest, copy

    for copy in loads[3:]:
        copy.start()

    def forward(h):
        for p, (A, B, C) in enumerate(AXES):
            for o in (1, 3):
                bsrc = (pos[B] + 4 - o) % 4
                piece = gs[p].at[bsrc, (h + pos[A] + bsrc) % 2, o // 2]
                take(piece, r2.at[p, h, o, o // 2])
                copy = remote(
                    piece, piece, f2.at[p, h, o], e2.at[p, h, o],
                    device(moved(pos, B, (pos[B] + o) % 4), core),
                )
                copy.start()
                forwards[p, h, o] = copy

    column = lax.broadcasted_iota(jnp.int32, (8 * 32, INFO), 1)
    drow = lax.broadcasted_iota(jnp.int32, (8 * 32, 1), 0)
    slot = drow % SLOTS
    source = lax.broadcasted_iota(jnp.int32, (1, 2 * TOK), 1)
    fits = ((drow % 32) // SLOTS == source // TOK) & (slot // CAP == (source // ROWS) % 2)
    wanted = (slot % CAP + 1).astype(F32)
    kept = {}
    for h in range(2):
        for j, b in enumerate((0,) + STEPS):
            if h == 0 and j in (1, 2):
                forward(j - 1)
            for p, (A, B, C) in enumerate(AXES):
                size = PARTS[p][1]
                if b == 2:
                    for o in (1, 3):
                        forwards[p, h, o].wait_recv()
                bsrc = (pos[B] + 4 - b) % 4
                low = (h + pos[A] + bsrc) % 2
                block = gs[p].at[bsrc, low]
                if b in (1, 3):
                    take(block.at[1 - b // 2], r2.at[p, h, b, 1 - b // 2])
                info = block[:, :, size:].reshape(2 * TOK, INFO)
                pick = (column == line_expert(pos, A, drow // 32)).astype(F32).astype(BF)
                places = lax.dot_general(
                    pick, info, (((1,), (1,)), ((), ())), preferred_element_type=F32
                )
                hot = jnp.where(fits & (places == wanted), 1.0, 0.0).astype(BF)
                picked = jnp.dot(
                    hot, block[:, :, :size].reshape(2 * TOK, size), preferred_element_type=F32
                ).astype(BF)
                ys[p][h, j] = picked.reshape(8, 2, SLOTS, size)
                for o in ORDER:
                    a = (pos[A] + o) % 4
                    for c in range(2):
                        sent = ys[p].at[h, j, 2 * a + (core + c) % 2]
                        target = half_rows(
                            xexp, h, (A, B, C), pos[A], bsrc, low, lanes_of(PARTS[p], core)
                        )
                        if o == 0 and c == 0:
                            copy = pltpu.make_async_copy(sent, target, loc.at[p, h, j])
                            kept[p, h, j] = copy
                        else:
                            copy = remote(
                                sent, target, s3.at[p, h, j], r3.at[p, h, j],
                                device(moved(pos, A, a), (core + c) % 2),
                            )
                        copy.start()
    for copies in (first_copies, early, forwards):
        for copy in copies.values():
            copy.wait_send()
    for rest, copy in second_copies.values():
        pl.when(rest)(copy.wait_send)

    back_kept = {}
    for h in range(2):
        for j in range(4):
            for p in range(3):
                kept[p, h, j].wait()
                take(ys[p].at[h, j, 0:7], r3.at[p, h, j])
        if h == 0:
            for copy in loads[3:]:
                copy.wait()

        @pl.loop(0, HIDDEN // 256)
        def _(n):
            cols = pl.ds(pl.multiple_of(n * 256, 256), 256)
            taken = xexp[h].reshape(512, WIDTH)
            gate_part = jnp.dot(taken, gate[:, cols], preferred_element_type=F32)
            up_part = jnp.dot(taken, up[:, cols], preferred_element_type=F32)
            act[:, cols] = (gate_part / (1.0 + jnp.exp(-gate_part)) * up_part).astype(BF)

        for p, (A, B, C) in enumerate(AXES):
            for c in (1, 0):
                lanes = lanes_of(BACK[p], (core + c) % 2)
                result = jnp.dot(act[...], down[:, lanes], preferred_element_type=F32).astype(BF)
                xexp[h, :, :, :, :, :, :, lanes] = result.reshape(
                    2, 2, 2, 2, 2, SLOTS, BACK[p][1]
                )
            for b in ORDER:
                bto = (pos[B] + b) % 4
                for o in ORDER:
                    a = (pos[A] + o) % 4
                    for c in (1, 0):
                        lanes = lanes_of(BACK[p], (core + c) % 2)
                        sent = half_rows(xexp, h, (A, B, C), a, bto, (h + a + bto) % 2, lanes)
                        target = qs[p].at[h, bto, 2 * pos[A] + core]
                        if o == 0 and c == 0:
                            copy = pltpu.make_async_copy(sent, target, bloc.at[p, h, b])
                            back_kept[p, h, b] = copy
                        else:
                            copy = remote(
                                sent, target, bs1.at[p, h, b], br1.at[p, h, b],
                                device(moved(pos, A, a), (core + c) % 2),
                            )
                        copy.start()

    entry = lax.broadcasted_iota(jnp.int32, (INFO, 8 * 32), 0)
    dcol = lax.broadcasted_iota(jnp.int32, (1, 8 * 32), 1)
    slot = dcol % SLOTS
    token = lax.broadcasted_iota(jnp.int32, (2 * TOK, 1), 0)
    fits = ((dcol % 32) // SLOTS == token // TOK) & (slot // CAP == (token // ROWS) % 2)
    wanted = (slot % CAP + 1).astype(F32)
    second_back = {}

    def weigh(h, b, p):
        A, B, C = AXES[p]
        size, back = PARTS[p][1], BACK[p][1]
        bto = (pos[B] + b) % 4
        back_kept[p, h, b].wait()
        take(qs[p].at[h, bto, 0:7], br1.at[p, h, b])
        info = gs[p].at[bto, (h + pos[A] + bto) % 2][:, :, size:].reshape(2 * TOK, INFO)
        expert = line_expert(pos, A, dcol // 32)
        places = jnp.dot(
            info, (entry == expert).astype(F32).astype(BF), preferred_element_type=F32
        )
        weights = jnp.dot(
            info, (entry == expert + SHARE).astype(F32).astype(BF), preferred_element_type=F32
        )
        hot = jnp.where(fits & (places == wanted), weights, 0.0).astype(BF)
        return jnp.dot(hot, qs[p][h, bto].reshape(8 * 32, back), preferred_element_type=F32)

    def pass_on(h, b, p, src, dst, which):
        to = device(moved(pos, AXES[p][1], (pos[AXES[p][1]] + b) % 4), core)
        copy = remote(src, dst, bs2.at[p, h, which], br2.at[p, h, which], to)
        copy.start()
        second_back[p, h, which] = copy

    for p in range(3):
        ts[p][0, 0, 2] = weigh(0, 2, p).astype(BF).reshape(2, TOK, BACK[p][1])
        pass_on(0, 1, p, ts[p].at[0, 0, 2, 0], ts[p].at[1, 0, 2, 0], 2)
        pass_on(0, 3, p, ts[p].at[0, 0, 2, 1], ts[p].at[1, 0, 2, 1], 0)
    for p in range(3):
        ts[p][0, 0, 0] = weigh(0, 0, p).astype(BF).reshape(2, TOK, BACK[p][1])
    for b in ORDER:
        for p in range(3):
            ts[p][0, 1, b] = weigh(1, b, p).astype(BF).reshape(2, TOK, BACK[p][1])
            if b:
                pass_on(1, b, p, ts[p].at[0, 1, b], ts[p].at[1, 1, b], b)
    for b, which in ((1, 2), (3, 0)):
        for p in range(3):
            high = b // 2
            block = weigh(0, b, p).reshape(2, TOK, BACK[p][1])
            second_back[p, 0, which].wait_recv()
            ts[p][0, 0, b, high] = (block[high] + ts[p][1, 0, 2, high].astype(F32)).astype(BF)
            ts[p][0, 0, b, 1 - high] = block[1 - high].astype(BF)
            pass_on(0, b, p, ts[p].at[0, 0, b], ts[p].at[1, 0, b], b)
    for h in (1, 0):
        for p, (A, B, C) in enumerate(AXES):
            total = ts[p][0, h, 0].astype(F32)
            for o in STEPS if h else (1, 3):
                second_back[p, h, o].wait_recv()
                total = total + ts[p][1, h, o].astype(F32)
            low = (h + pos[A] + pos[B]) % 2
            us[p][low] = total.astype(BF)
            for high in range(2):
                cto = 2 * high + low
                o = (cto + 4 - pos[C]) % 4
                for c in (1, 0):
                    to = (core + c) % 2
                    copy = remote(
                        us[p].at[low, high, pl.ds(pl.multiple_of(to * ROWS, ROWS), ROWS)],
                        vs[p].at[o, c], bs3.at[p, o, c], br3.at[p, o, c],
                        device(moved(pos, C, cto), to),
                    )
                    if c:
                        copy.start()
                    else:
                        pl.when(o != 0)(copy.start)
    for p, (A, B, C) in enumerate(AXES):
        vs[p][0, 0] = us[p][pos[C] % 2, pos[C] // 2, rows]
        for c in range(2):
            total = jnp.zeros((ROWS, BACK[p][1]), F32)
            for o in range(4):
                if o or c:
                    take(vs[p].at[o, c], br3.at[p, o, c])
                total = total + vs[p][o, c].astype(F32)
            out[:, lanes_of(BACK[p], (core + c) % 2)] = total.astype(BF)
    for p in range(3):
        for o in range(4):
            for c in range(2):
                if o or c:
                    take(vs[p].at[o, c], bs3.at[p, o, c])
    for h in range(2):
        for p in range(3):
            for j in range(4):
                take(ys[p].at[h, j, 0:7], s3.at[p, h, j])
                take(qs[p].at[h, j, 0:7], bs1.at[p, h, j])
    for copy in second_back.values():
        copy.wait_send()


def vmem(*shape):
    return pltpu.VMEM(shape, BF)


def dma(*shape):
    return pltpu.SemaphoreType.DMA(shape)


def on_device(hidden_in, routes, scores, w_gate, w_up, w_down):
    sizes = [size for _, size in PARTS]
    backs = [size for _, size in BACK]
    top = routes.shape[1]
    anywhere = pl.BlockSpec(memory_space=pl.ANY)
    return pl.pallas_call(
        kernel,
        out_shape=pltpu.VMEM((ROWS, WIDTH), BF),
        in_specs=[anywhere] * 6,
        out_specs=pl.BlockSpec(memory_space=pltpu.VMEM),
        scratch_shapes=[vmem(ROWS, WIDTH)]
        + [pltpu.VMEM((top, ROWS), jnp.int32), pltpu.VMEM((top, ROWS), F32)]
        + [vmem(WIDTH, HIDDEN), vmem(WIDTH, HIDDEN), vmem(HIDDEN, WIDTH)]
        + [vmem(2, ROWS, size + INFO) for size in sizes]
        + [vmem(4, 2, 2, TOK, size + INFO) for size in sizes]
        + [vmem(2, 4, 8, 2, SLOTS, size) for size in sizes]
        + [vmem(2, 2, 2, 2, 2, 2, SLOTS, WIDTH), vmem(512, HIDDEN)]
        + [vmem(2, 4, 8, 2, SLOTS, size) for size in backs]
        + [vmem(2, 2, 4, 2, TOK, size) for size in backs]
        + [vmem(2, 2, TOK, size) for size in backs]
        + [vmem(4, 2, ROWS, size) for size in backs]
        + [dma(6), dma(3, 4, 2), dma(3, 4, 2)]
        + [dma(3, 4, 2), dma(3, 2, 4, 2), dma(3, 2, 4, 2)]
        + [dma(3, 2, 4)] * 10
        + [dma(3, 4, 2), dma(3, 4, 2)],
        compiler_params=pltpu.CompilerParams(
            collective_id=0, has_side_effects=True, vmem_limit_bytes=62_500_000
        ),
        name="experts",
    )(hidden_in, routes.T, scores.T, w_gate, w_up, w_down)


def solution(mesh):
    placed = (
        P(("sec", "dev"), None),
        P(("sec", "dev"), None),
        P(("sec", "dev"), None),
        P("dev", None, "sec"),
        P("dev", None, "sec"),
        P("dev", "sec", None),
    )
    return jax.shard_map(
        on_device, mesh=mesh, in_specs=placed, out_specs=P(("sec", "dev"), None), check_vma=False
    )
```

```python
import jax
import jax.numpy as jnp
from jax import lax
from jax.experimental import pallas as pl
from jax.experimental.pallas import tpu as pltpu
from jax.sharding import PartitionSpec as P

MESH = pl.DeviceIdType.MESH
BF = jnp.bfloat16
F32 = jnp.float32

ROWS = 32
WIDTH = 4096
HALF = WIDTH // 2
HIDDEN = 768
CAP = 8
SLOTS = 2 * CAP
TOK = 2 * ROWS
INFO = 128
SHARE = 64
AXES = ((0, 1, 2), (1, 2, 0), (2, 0, 1))
PARTS = ((0, 640), (640, 640), (1280, 768))
BACK = ((0, 768), (768, 640), (1408, 640))
STEPS = (1, 3, 2)
ORDER = (2, 1, 3, 0)


def where_am_i():
    dev = lax.axis_index("dev")
    sec = lax.axis_index("sec")
    core = dev % 2
    z = (dev // 2) % 4
    y = ((dev // 8) % 2) * 2 + sec
    x = dev // 16
    return (x, y, z), core


def expert_of(x, y, z, core):
    return ((x * 2 + y // 2) * 4 + z) * 2 + core


def device(pos, core):
    x, y, z = pos
    return {"sec": y % 2, "dev": expert_of(x, y, z, core)}


def moved(pos, axis, to):
    return tuple(to if i == axis else v for i, v in enumerate(pos))


def greet(pos, core):
    barrier = pltpu.get_barrier_semaphore()
    count = 1
    pl.semaphore_signal(barrier, inc=1, device_id=device(pos, 1 - core), device_id_type=MESH)
    for axis in range(3):
        for o in STEPS:
            for c in range(2):
                to = device(moved(pos, axis, (pos[axis] + o) % 4), (core + c) % 2)
                pl.semaphore_signal(barrier, inc=1, device_id=to, device_id_type=MESH)
                count += 1
    return count


def remote(src, dst, send, recv, to):
    return pltpu.make_async_remote_copy(
        src_ref=src, dst_ref=dst, send_sem=send, recv_sem=recv, device_id=to, device_id_type=MESH
    )


def take(ref, sem):
    pltpu.make_async_copy(ref, ref, sem).wait()


def line_expert(pos, axis, d):
    place, core = d // 2, d % 2
    x, y, z = moved(pos, axis, place)
    return expert_of(x, y, z, core)


def half_rows(ref, h, axes, a, b, low, lanes):
    A, B, C = axes
    high, bit = [None] * 3, [None] * 3
    for axis, v in ((A, a), (B, b)):
        high[axis], bit[axis] = v // 2, v % 2
    high[C], bit[C] = slice(None), low
    return ref.at[h, high[0], bit[0], high[1], bit[1], high[2], :, lanes]


def lanes_of(part, core):
    first, size = part
    return pl.ds(pl.multiple_of(core * HALF + first, 128), size)


def kernel(
    hidden, routes, scores, w_gate, w_up, w_down, out,
    hid, rt, sc, gate, up, down, m0, m1, m2,
    g0, g1, g2, y0, y1, y2, xexp, act,
    q0, q1, q2, t0, t1, t2, u0, u1, u2, v0, v1, v2,
    ld, s1, r1, es, s2, r2, f2, e2, s3, r3, loc, bs1, br1, bloc, bs2, br2, bs3, br3,
):
    pos, core = where_am_i()
    ms, gs, ys, qs = (m0, m1, m2), (g0, g1, g2), (y0, y1, y2), (q0, q1, q2)
    ts, us, vs = (t0, t1, t2), (u0, u1, u2), (v0, v1, v2)
    loads = [
        pltpu.make_async_copy(src, dst, ld.at[i])
        for i, (src, dst) in enumerate(
            (
                (hidden, hid), (routes, rt), (scores, sc),
                (w_gate.at[0], gate), (w_up.at[0], up), (w_down.at[0], down),
            )
        )
    ]
    for copy in loads[:3]:
        copy.start()
    peers = greet(pos, core)
    for copy in loads[1:3]:
        copy.wait()

    share = sc[...] / jnp.sum(sc[...], 0, keepdims=True)
    chosen = rt[...]
    entry = lax.broadcasted_iota(jnp.int32, (INFO, ROWS), 0)
    used = jnp.zeros((INFO, ROWS), F32)
    shares = jnp.zeros((INFO, ROWS), F32)
    for k in range(chosen.shape[0]):
        e = chosen[k : k + 1]
        used = used + jnp.where(entry == e, 1.0, 0.0)
        shares = shares + jnp.where(entry == e + SHARE, share[k : k + 1], 0.0)
    ahead = lax.broadcasted_iota(jnp.int32, (ROWS, ROWS), 0)
    behind = lax.broadcasted_iota(jnp.int32, (ROWS, ROWS), 1)
    place = jnp.dot(
        used.astype(BF), (ahead < behind).astype(F32).astype(BF), preferred_element_type=F32
    )
    table = jnp.where(entry < SHARE, used * (place + 1.0), shares).astype(BF)
    mine = lax.dot_general(
        (ahead == behind).astype(F32).astype(BF), table, (((1,), (1,)), ((), ())),
        preferred_element_type=F32,
    ).astype(BF)
    loads[0].wait()
    values = hid[...].astype(F32)
    scale = lax.rsqrt(jnp.mean(values * values, -1, keepdims=True) + 1e-06)
    normed = (values * scale).astype(BF)
    for p, (first, size) in enumerate(PARTS):
        for c in range(2):
            ms[p][c, :, :size] = normed[:, c * HALF + first : c * HALF + first + size]
            ms[p][c, :, size:] = mine
    pl.semaphore_wait(pltpu.get_barrier_semaphore(), peers)

    rows = pl.ds(pl.multiple_of(core * ROWS, ROWS), ROWS)
    first_copies, early, second_copies, forwards = {}, {}, {}, {}
    for p, (A, B, C) in enumerate(AXES):
        own = gs[p].at[pos[B], pos[C] % 2, pos[C] // 2, rows]
        for o in (2, 1, 3, 0):
            for c in range(2):
                if o or c:
                    copy = remote(
                        ms[p].at[(core + c) % 2], own, s1.at[p, o, c], r1.at[p, o, c],
                        device(moved(pos, C, (pos[C] + o) % 4), (core + c) % 2),
                    )
                    copy.start()
                    first_copies[p, o, c] = copy
        own[...] = ms[p][core]
    for p, (A, B, C) in enumerate(AXES):
        own = gs[p].at[pos[B], pos[C] % 2, pos[C] // 2, rows]
        h = (pos[A] + pos[B] + pos[C]) % 2
        for o in (1, 3):
            for c in range(2):
                copy = remote(
                    ms[p].at[(core + c) % 2], own, es.at[p, o, c], r2.at[p, h, o, pos[C] // 2],
                    device(moved(pos, B, (pos[B] + o) % 4), (core + c) % 2),
                )
                copy.start()
                early[p, o, c] = copy
    for p, (A, B, C) in enumerate(AXES):
        for o in range(4):
            for c in range(2):
                if o or c:
                    first_copies[p, o, c].wait_recv()
        for h in range(2):
            low = (h + pos[A] + pos[B]) % 2
            for o in (1, 3):
                for high in range(2):
                    block = gs[p].at[pos[B], low, high]
                    copy = remote(
                        block, block, s2.at[p, h, o, high], r2.at[p, h, o, high],
                        device(moved(pos, B, (pos[B] + o) % 4), core),
                    )
                    rest = 2 * high + low != pos[C]
                    pl.when(rest)(copy.start)
                    second_copies[p, h, o, high] = rest, copy

    for copy in loads[3:]:
        copy.start()

    def forward(h):
        for p, (A, B, C) in enumerate(AXES):
            for o in (1, 3):
                bsrc = (pos[B] + 4 - o) % 4
                piece = gs[p].at[bsrc, (h + pos[A] + bsrc) % 2, o // 2]
                take(piece, r2.at[p, h, o, o // 2])
                copy = remote(
                    piece, piece, f2.at[p, h, o], e2.at[p, h, o],
                    device(moved(pos, B, (pos[B] + o) % 4), core),
                )
                copy.start()
                forwards[p, h, o] = copy

    column = lax.broadcasted_iota(jnp.int32, (8 * 32, INFO), 1)
    drow = lax.broadcasted_iota(jnp.int32, (8 * 32, 1), 0)
    slot = drow % SLOTS
    source = lax.broadcasted_iota(jnp.int32, (1, 2 * TOK), 1)
    fits = ((drow % 32) // SLOTS == source // TOK) & (slot // CAP == (source // ROWS) % 2)
    wanted = (slot % CAP + 1).astype(F32)
    kept = {}
    for h in range(2):
        for j, b in enumerate((0,) + STEPS):
            if h == 0 and j in (1, 2):
                forward(j - 1)
            for p, (A, B, C) in enumerate(AXES):
                size = PARTS[p][1]
                if b == 2:
                    for o in (1, 3):
                        forwards[p, h, o].wait_recv()
                bsrc = (pos[B] + 4 - b) % 4
                low = (h + pos[A] + bsrc) % 2
                block = gs[p].at[bsrc, low]
                if b in (1, 3):
                    take(block.at[1 - b // 2], r2.at[p, h, b, 1 - b // 2])
                info = block[:, :, size:].reshape(2 * TOK, INFO)
                pick = (column == line_expert(pos, A, drow // 32)).astype(F32).astype(BF)
                places = lax.dot_general(
                    pick, info, (((1,), (1,)), ((), ())), preferred_element_type=F32
                )
                hot = jnp.where(fits & (places == wanted), 1.0, 0.0).astype(BF)
                picked = jnp.dot(
                    hot, block[:, :, :size].reshape(2 * TOK, size), preferred_element_type=F32
                ).astype(BF)
                ys[p][h, j] = picked.reshape(8, 2, SLOTS, size)
                for o in ORDER:
                    a = (pos[A] + o) % 4
                    for c in range(2):
                        sent = ys[p].at[h, j, 2 * a + (core + c) % 2]
                        target = half_rows(
                            xexp, h, (A, B, C), pos[A], bsrc, low, lanes_of(PARTS[p], core)
                        )
                        if o == 0 and c == 0:
                            copy = pltpu.make_async_copy(sent, target, loc.at[p, h, j])
                            kept[p, h, j] = copy
                        else:
                            copy = remote(
                                sent, target, s3.at[p, h, j], r3.at[p, h, j],
                                device(moved(pos, A, a), (core + c) % 2),
                            )
                        copy.start()
    for copies in (first_copies, early, forwards):
        for copy in copies.values():
            copy.wait_send()
    for rest, copy in second_copies.values():
        pl.when(rest)(copy.wait_send)

    back_kept = {}
    entry = lax.broadcasted_iota(jnp.int32, (INFO, 8 * 32), 0)
    dcol = lax.broadcasted_iota(jnp.int32, (1, 8 * 32), 1)
    slot = dcol % SLOTS
    token = lax.broadcasted_iota(jnp.int32, (2 * TOK, 1), 0)
    fits = ((dcol % 32) // SLOTS == token // TOK) & (slot // CAP == (token // ROWS) % 2)
    wanted = (slot % CAP + 1).astype(F32)
    second_back = {}

    def weigh(h, b, p):
        A, B, C = AXES[p]
        size, back = PARTS[p][1], BACK[p][1]
        bto = (pos[B] + b) % 4
        back_kept[p, h, b].wait()
        take(qs[p].at[h, bto, 0:7], br1.at[p, h, b])
        info = gs[p].at[bto, (h + pos[A] + bto) % 2][:, :, size:].reshape(2 * TOK, INFO)
        expert = line_expert(pos, A, dcol // 32)
        places = jnp.dot(
            info, (entry == expert).astype(F32).astype(BF), preferred_element_type=F32
        )
        weights = jnp.dot(
            info, (entry == expert + SHARE).astype(F32).astype(BF), preferred_element_type=F32
        )
        hot = jnp.where(fits & (places == wanted), weights, 0.0).astype(BF)
        return jnp.dot(hot, qs[p][h, bto].reshape(8 * 32, back), preferred_element_type=F32)

    def pass_on(h, b, p, src, dst, which):
        to = device(moved(pos, AXES[p][1], (pos[AXES[p][1]] + b) % 4), core)
        copy = remote(src, dst, bs2.at[p, h, which], br2.at[p, h, which], to)
        copy.start()
        second_back[p, h, which] = copy

    for h in range(2):
        for j in range(4):
            for p in range(3):
                kept[p, h, j].wait()
                take(ys[p].at[h, j, 0:7], r3.at[p, h, j])
        if h == 0:
            for copy in loads[3:]:
                copy.wait()

        @pl.loop(0, HIDDEN // 256)
        def _(n):
            cols = pl.ds(pl.multiple_of(n * 256, 256), 256)
            taken = xexp[h].reshape(512, WIDTH)
            gate_part = jnp.dot(taken, gate[:, cols], preferred_element_type=F32)
            up_part = jnp.dot(taken, up[:, cols], preferred_element_type=F32)
            act[:, cols] = (gate_part / (1.0 + jnp.exp(-gate_part)) * up_part).astype(BF)

        if h == 1:
            for p in range(3):
                ts[p][0, 0, 2] = weigh(0, 2, p).astype(BF).reshape(2, TOK, BACK[p][1])
                pass_on(0, 1, p, ts[p].at[0, 0, 2, 0], ts[p].at[1, 0, 2, 0], 2)
                pass_on(0, 3, p, ts[p].at[0, 0, 2, 1], ts[p].at[1, 0, 2, 1], 0)
        for p, (A, B, C) in enumerate(AXES):
            for c in (1, 0):
                lanes = lanes_of(BACK[p], (core + c) % 2)
                result = jnp.dot(act[...], down[:, lanes], preferred_element_type=F32).astype(BF)
                xexp[h, :, :, :, :, :, :, lanes] = result.reshape(
                    2, 2, 2, 2, 2, SLOTS, BACK[p][1]
                )
            for b in ORDER:
                bto = (pos[B] + b) % 4
                for o in ORDER:
                    a = (pos[A] + o) % 4
                    for c in (1, 0):
                        lanes = lanes_of(BACK[p], (core + c) % 2)
                        sent = half_rows(xexp, h, (A, B, C), a, bto, (h + a + bto) % 2, lanes)
                        target = qs[p].at[h, bto, 2 * pos[A] + core]
                        if o == 0 and c == 0:
                            copy = pltpu.make_async_copy(sent, target, bloc.at[p, h, b])
                            back_kept[p, h, b] = copy
                        else:
                            copy = remote(
                                sent, target, bs1.at[p, h, b], br1.at[p, h, b],
                                device(moved(pos, A, a), (core + c) % 2),
                            )
                        copy.start()

    for p in range(3):
        ts[p][0, 0, 0] = weigh(0, 0, p).astype(BF).reshape(2, TOK, BACK[p][1])
    for b, which in ((1, 2), (3, 0)):
        for p in range(3):
            high = b // 2
            block = weigh(0, b, p).reshape(2, TOK, BACK[p][1])
            second_back[p, 0, which].wait_recv()
            ts[p][0, 0, b, high] = (block[high] + ts[p][1, 0, 2, high].astype(F32)).astype(BF)
            ts[p][0, 0, b, 1 - high] = block[1 - high].astype(BF)
            pass_on(0, b, p, ts[p].at[0, 0, b], ts[p].at[1, 0, b], b)
    for b in ORDER:
        for p in range(3):
            ts[p][0, 1, b] = weigh(1, b, p).astype(BF).reshape(2, TOK, BACK[p][1])
            if b:
                pass_on(1, b, p, ts[p].at[0, 1, b], ts[p].at[1, 1, b], b)
    for h in (0, 1):
        for p, (A, B, C) in enumerate(AXES):
            total = ts[p][0, h, 0].astype(F32)
            for o in STEPS if h else (1, 3):
                second_back[p, h, o].wait_recv()
                total = total + ts[p][1, h, o].astype(F32)
            low = (h + pos[A] + pos[B]) % 2
            us[p][low] = total.astype(BF)
            for high in range(2):
                cto = 2 * high + low
                o = (cto + 4 - pos[C]) % 4
                for c in (1, 0):
                    to = (core + c) % 2
                    copy = remote(
                        us[p].at[low, high, pl.ds(pl.multiple_of(to * ROWS, ROWS), ROWS)],
                        vs[p].at[o, c], bs3.at[p, o, c], br3.at[p, o, c],
                        device(moved(pos, C, cto), to),
                    )
                    if c:
                        copy.start()
                    else:
                        pl.when(o != 0)(copy.start)
    for p, (A, B, C) in enumerate(AXES):
        vs[p][0, 0] = us[p][pos[C] % 2, pos[C] // 2, rows]
        for c in range(2):
            total = jnp.zeros((ROWS, BACK[p][1]), F32)
            for o in range(4):
                if o or c:
                    take(vs[p].at[o, c], br3.at[p, o, c])
                total = total + vs[p][o, c].astype(F32)
            out[:, lanes_of(BACK[p], (core + c) % 2)] = total.astype(BF)
    for p in range(3):
        for o in range(4):
            for c in range(2):
                if o or c:
                    take(vs[p].at[o, c], bs3.at[p, o, c])
    for h in range(2):
        for p in range(3):
            for j in range(4):
                take(ys[p].at[h, j, 0:7], s3.at[p, h, j])
                take(qs[p].at[h, j, 0:7], bs1.at[p, h, j])
    for copy in second_back.values():
        copy.wait_send()


def vmem(*shape):
    return pltpu.VMEM(shape, BF)


def dma(*shape):
    return pltpu.SemaphoreType.DMA(shape)


def on_device(hidden_in, routes, scores, w_gate, w_up, w_down):
    sizes = [size for _, size in PARTS]
    backs = [size for _, size in BACK]
    top = routes.shape[1]
    anywhere = pl.BlockSpec(memory_space=pl.ANY)
    return pl.pallas_call(
        kernel,
        out_shape=pltpu.VMEM((ROWS, WIDTH), BF),
        in_specs=[anywhere] * 6,
        out_specs=pl.BlockSpec(memory_space=pltpu.VMEM),
        scratch_shapes=[vmem(ROWS, WIDTH)]
        + [pltpu.VMEM((top, ROWS), jnp.int32), pltpu.VMEM((top, ROWS), F32)]
        + [vmem(WIDTH, HIDDEN), vmem(WIDTH, HIDDEN), vmem(HIDDEN, WIDTH)]
        + [vmem(2, ROWS, size + INFO) for size in sizes]
        + [vmem(4, 2, 2, TOK, size + INFO) for size in sizes]
        + [vmem(2, 4, 8, 2, SLOTS, size) for size in sizes]
        + [vmem(2, 2, 2, 2, 2, 2, SLOTS, WIDTH), vmem(512, HIDDEN)]
        + [vmem(2, 4, 8, 2, SLOTS, size) for size in backs]
        + [vmem(2, 2, 4, 2, TOK, size) for size in backs]
        + [vmem(2, 2, TOK, size) for size in backs]
        + [vmem(4, 2, ROWS, size) for size in backs]
        + [dma(6), dma(3, 4, 2), dma(3, 4, 2)]
        + [dma(3, 4, 2), dma(3, 2, 4, 2), dma(3, 2, 4, 2)]
        + [dma(3, 2, 4)] * 10
        + [dma(3, 4, 2), dma(3, 4, 2)],
        compiler_params=pltpu.CompilerParams(
            collective_id=0, has_side_effects=True, vmem_limit_bytes=64_000_000
        ),
        name="experts",
    )(hidden_in, routes.T, scores.T, w_gate, w_up, w_down)


def solution(mesh):
    placed = (
        P(("sec", "dev"), None),
        P(("sec", "dev"), None),
        P(("sec", "dev"), None),
        P("dev", None, "sec"),
        P("dev", None, "sec"),
        P("dev", "sec", None),
    )
    return jax.shard_map(
        on_device, mesh=mesh, in_specs=placed, out_specs=P(("sec", "dev"), None), check_vma=False
    )
```
